32 devices in a mesh: slab: 8 (over y, x, core), grp: 4 (over z).
Axes of the slice: x: 2, y: 2, z: 4, core: 2. Of those that a mesh axis runs over, the one named last changes fastest.
Arguments:
- near_field: bfloat16 [2, 4096, 2048], P(None, 'slab', 'grp'), may hold values from -6 to 6
- lens_phase: float32 [2, 4096, 2048], P(None, 'slab', 'grp'), may hold values from -3.140625 to 3.140625
Outputs:
- far_field: float32 [2, 512, 2048], P(None, ('slab', 'grp'))
The draws below stay inside these ranges and needn't reach their ends.
All inputs are finite; a program needn't handle non-finite values.
Results may differ from the reference program's by a relative error of at most 0.0083.
Values may be sent and summed in bfloat16 or wider, within the bound.
A program may use at most 128 MiB of HBM per device.

```python
import math
import jax
import jax.numpy as jnp
from jax import lax

NV = 2048
AV = 512
AL = 2048
STEPS = 2
LAT_DEV = 512
NL = 4096
N_SLAB = 8


def level_of(stream_key, shape, split, smallest, high):
    level = 1.0
    for dim, parts in split:
        heights = jax.random.uniform(jax.random.fold_in(jax.random.fold_in(stream_key, 6), dim), (parts,), jnp.float32, smallest / len(split), high / len(split))
        level = level * jnp.repeat(jnp.exp(heights), shape[dim] // parts).reshape((-1,) + (1,) * (len(shape) - 1 - dim))
    return level


def normal_values(own_key, shape, deviation, bound, shards=(), kind=jnp.bfloat16):
    level = level_of(own_key, shape, shards, -0.22, 0.18) if shards else 1.0
    result = jax.random.normal(own_key, shape, jnp.float32) * deviation * level
    return jnp.minimum(jnp.maximum(result, -bound), bound).astype(kind)


def setup_inputs(seed: int = 0) -> dict:
    splits = jax.random.split(jax.random.key(seed), 3)
    return {
        "near_field": normal_values(splits[0], (2, NL, NV), 1.0, 6.0, ((1, 8), (2, 4))),
        "lens_phase": jnp.clip(jax.random.uniform(splits[1], (STEPS, NL, NV), jnp.float32, -3.140625, 3.140625), -3.140625, 3.140625),
    }


def phase_table(row_index, col_index, modulus):
    turns = jnp.mod(row_index[:, None] * col_index[None, :], modulus)
    angle = turns.astype(jnp.float32) * (2.0 * math.pi / modulus)
    return (jnp.cos(angle).astype(jnp.bfloat16), jnp.sin(angle).astype(jnp.bfloat16))

def propagator():
    wave_index = jnp.arange(NV, dtype=jnp.int32)
    offset = wave_index[None, :] - wave_index[:, None]
    turns = jnp.mod(offset * offset, 2 * NV)
    angle = turns.astype(jnp.float32) * (math.pi / NV) - math.pi / 4.0
    gain = 1.0 / math.sqrt(NV)
    return ((jnp.cos(angle) * gain).astype(jnp.bfloat16), (jnp.sin(angle) * gain).astype(jnp.bfloat16))

def matmul(left, right):
    return jnp.dot(left.astype(jnp.float32), right.astype(jnp.float32), precision=lax.Precision.HIGHEST)

def reference(near_field, lens_phase):
    total_rows = LAT_DEV * N_SLAB
    wave_index = jnp.arange(NV, dtype=jnp.int32)
    prop_cos, prop_sin = propagator()
    real_part = near_field[0]
    imag_part = near_field[1]
    for section in range(STEPS):
        prop_real = (matmul(real_part, prop_cos) - matmul(imag_part, prop_sin)).astype(jnp.bfloat16)
        prop_imag = (matmul(real_part, prop_sin) + matmul(imag_part, prop_cos)).astype(jnp.bfloat16)
        lens_cos = jnp.cos(lens_phase[section])
        lens_sin = jnp.sin(lens_phase[section])
        prop_real = prop_real.astype(jnp.float32)
        prop_imag = prop_imag.astype(jnp.float32)
        real_part = (prop_real * lens_cos - prop_imag * lens_sin).astype(jnp.bfloat16)
        imag_part = (prop_real * lens_sin + prop_imag * lens_cos).astype(jnp.bfloat16)
    vert_cos, vert_sin = phase_table(wave_index - NV // 2, jnp.arange(AV, dtype=jnp.int32) - AV // 2, 2 * NV)
    col_real = (matmul(real_part, vert_cos) + matmul(imag_part, vert_sin)).astype(jnp.bfloat16)
    col_imag = (matmul(imag_part, vert_cos) - matmul(real_part, vert_sin)).astype(jnp.bfloat16)
    lat_cos, lat_sin = phase_table(jnp.arange(total_rows, dtype=jnp.int32) - total_rows // 2, jnp.arange(AL, dtype=jnp.int32) - AL // 2, 2 * total_rows)
    lat_cos = lat_cos.astype(jnp.float32)
    lat_sin = lat_sin.astype(jnp.float32)
    col_real = col_real.astype(jnp.float32)
    col_imag = col_imag.astype(jnp.float32)
    hp = lax.Precision.HIGHEST
    out_real = jnp.einsum('na,nj->aj', col_real, lat_cos, precision=hp) + jnp.einsum('na,nj->aj', col_imag, lat_sin, precision=hp)
    out_imag = jnp.einsum('na,nj->aj', col_imag, lat_cos, precision=hp) - jnp.einsum('na,nj->aj', col_real, lat_sin, precision=hp)
    scale = 1.0 / math.sqrt(total_rows * NV)
    return jnp.stack([out_real, out_imag]) * scale
```

```python
import math

import jax
import jax.numpy as jnp
from jax import lax
from jax.experimental import pallas as pl
from jax.experimental.pallas import tpu as pltpu
from jax.sharding import PartitionSpec as P

AV = 512
AL = 2048
PHASE_CODE = 40.0


def sincos(angle):
    half = 0.5 * angle
    sq = half * half
    sin = -1.0 / 39916800.0
    for term in (1.0 / 362880.0, -1.0 / 5040.0, 1.0 / 120.0, -1.0 / 6.0, 1.0):
        sin = sin * sq + term
    sin = sin * half
    cos = 1.0 / 479001600.0
    for term in (-1.0 / 3628800.0, 1.0 / 40320.0, -1.0 / 720.0, 1.0 / 24.0, -0.5, 1.0):
        cos = cos * sq + term
    return 1.0 - 2.0 * sin * sin, 2.0 * sin * cos


def unit_angle(turns, modulus):
    assert modulus & (modulus - 1) == 0
    centred = ((turns + modulus // 2) & (modulus - 1)) - modulus // 2
    return sincos(centred.astype(jnp.float32) * (2.0 * math.pi / modulus))


def count(size):
    return lax.optimization_barrier(jnp.arange(size, dtype=jnp.int32))


def phase_table(row_index, col_index, modulus):
    cos, sin = unit_angle(row_index[:, None] * col_index[None, :], modulus)
    return cos.astype(jnp.bfloat16), sin.astype(jnp.bfloat16)


def conjugate(table):
    cos, sin = table
    return jnp.stack([jnp.stack([cos, -sin]), jnp.stack([sin, cos])])


def propagator(points):
    band = math.gcd(points, 256)
    offset = count(points)[None, :] - count(band)[:, None]
    cos, sin = unit_angle(offset * offset - points // 4, 2 * points)
    gain = 1.0 / math.sqrt(points)

    def rolled(part):
        part = lax.optimization_barrier((part * gain).astype(jnp.bfloat16))
        twice = jnp.concatenate([part, part], axis=1)
        return jnp.concatenate(
            [
                lax.slice_in_dim(twice, points - start, 2 * points - start, axis=1)
                for start in range(0, points, band)
            ]
        )

    return rolled(cos), rolled(sin)


def matmul(left, right):
    return jnp.dot(left, right, preferred_element_type=jnp.float32)


def complex_product(both, table_cos, table_sin):
    rows = both.shape[0] // 2
    with_cos = matmul(both, table_cos)
    with_sin = matmul(both, table_sin)
    return with_cos[:rows] - with_sin[rows:], with_sin[:rows] + with_cos[rows:]


def exchange_kernel(groups, devices, source, target, send_sem, recv_sem, own_sem):
    me = lax.axis_index("slab") * groups + lax.axis_index("grp")
    barrier = pltpu.get_barrier_semaphore()

    def place(device):
        return (lax.div(device, groups), lax.rem(device, groups))

    def greet(step, carry):
        peer = lax.rem(me + step, devices)
        pl.semaphore_signal(
            barrier, inc=1, device_id=place(peer), device_id_type=pl.DeviceIdType.MESH
        )
        return carry

    lax.fori_loop(1, devices, greet, 0)
    pl.semaphore_wait(barrier, devices - 1)

    def block(step):
        peer = lax.rem(me + step, devices)
        return pltpu.make_async_remote_copy(
            src_ref=source.at[peer],
            dst_ref=target.at[me],
            send_sem=send_sem.at[step],
            recv_sem=recv_sem.at[step],
            device_id=place(peer),
            device_id_type=pl.DeviceIdType.MESH,
        )

    def send(step, carry):
        block(step).start()
        return carry

    def wait(step, carry):
        block(step).wait()
        return carry

    lax.fori_loop(1, devices, send, 0)
    own = pltpu.make_async_copy(source.at[me], target.at[me], own_sem)
    own.start()
    own.wait()
    lax.fori_loop(1, devices, wait, 0)


def exchange(blocks, groups):
    devices = blocks.shape[0]

    def kernel(*refs):
        exchange_kernel(groups, devices, *refs)

    return pl.pallas_call(
        kernel,
        out_shape=jax.ShapeDtypeStruct(blocks.shape, blocks.dtype),
        in_specs=[pl.BlockSpec(memory_space=pltpu.VMEM)],
        out_specs=pl.BlockSpec(memory_space=pltpu.VMEM),
        scratch_shapes=[
            pltpu.SemaphoreType.DMA((devices,)),
            pltpu.SemaphoreType.DMA((devices,)),
            pltpu.SemaphoreType.DMA,
        ],
        compiler_params=pltpu.CompilerParams(collective_id=0, has_side_effects=True),
        name="column_exchange",
    )(blocks)


def on_device(near_field, lens_phase):
    slab_count = lax.axis_size("slab")
    group_count = lax.axis_size("grp")
    devices = slab_count * group_count
    steps, lat_dev, width = lens_phase.shape
    points = width * group_count
    total_rows = lat_dev * slab_count
    rows = lat_dev // group_count
    angles = AV // devices
    coded = [jnp.exp2(lens_phase[k] * PHASE_CODE).astype(jnp.bfloat16) for k in range(steps)]
    blocks = jnp.transpose(near_field.reshape(2, group_count, rows, width), (1, 0, 2, 3))
    field = lax.all_to_all(blocks, "grp", split_axis=0, concat_axis=0, tiled=True)
    arrived = field
    moved = []
    for part in coded:
        part, arrived = lax.optimization_barrier((part, arrived))
        if not moved:
            field = arrived
        else:
            moved[-1] = arrived
        arrived = lax.all_to_all(part, "grp", split_axis=0, concat_axis=1, tiled=True)
        moved.append(arrived)
    coded = moved
    prop_cos, prop_sin = propagator(points)
    both = jnp.transpose(field, (1, 2, 0, 3)).reshape(2 * rows, points)
    for section in range(steps):
        real, imag = complex_product(both, prop_cos, prop_sin)
        real = real.astype(jnp.bfloat16).astype(jnp.float32)
        imag = imag.astype(jnp.bfloat16).astype(jnp.float32)
        phase = jnp.log2(coded[section].astype(jnp.float32)) * (1.0 / PHASE_CODE)
        lens_cos, lens_sin = sincos(phase)
        both = jnp.concatenate(
            [
                (real * lens_cos - imag * lens_sin).astype(jnp.bfloat16),
                (real * lens_sin + imag * lens_cos).astype(jnp.bfloat16),
            ]
        )
    vert_cos, vert_sin = phase_table(
        count(AV) - AV // 2, count(points) - points // 2, 2 * points
    )
    vert_cos, vert_sin = lax.optimization_barrier((vert_cos, vert_sin))
    with_cos = jnp.einsum("av,nv->an", vert_cos, both, preferred_element_type=jnp.float32)
    with_sin = jnp.einsum("av,nv->an", vert_sin, both, preferred_element_type=jnp.float32)
    col_real = (with_cos[:, :rows] + with_sin[:, rows:]).astype(jnp.bfloat16)
    col_imag = (with_cos[:, rows:] - with_sin[:, :rows]).astype(jnp.bfloat16)
    cols = jnp.stack([part.reshape(devices, angles, rows) for part in (col_real, col_imag)], axis=1)
    got = exchange(cols.reshape(devices, 2 * angles, rows), group_count)
    modulus = 2 * total_rows
    period = modulus // rows
    source = count(devices) - devices // 2
    fine = count(period)
    near = count(rows)
    coarse = count(AL // period)
    scale = 1.0 / math.sqrt(total_rows * points)
    got = got.reshape(devices, 2, angles, rows)
    weights = conjugate(phase_table(source, fine, period))
    mid = jnp.einsum("skam,kcsf->cafm", got, weights, preferred_element_type=jnp.float32)
    t_cos, t_sin = unit_angle(fine[:, None] * near[None, :], modulus)
    t_cos = t_cos * scale
    t_sin = t_sin * scale
    turned = jnp.stack([mid[0] * t_cos + mid[1] * t_sin, mid[1] * t_cos - mid[0] * t_sin])
    weights = conjugate(phase_table(near, coarse * period - AL // 2, modulus))
    out = jnp.einsum(
        "kafm,kcmd->cadf", turned.astype(jnp.bfloat16), weights, preferred_element_type=jnp.float32
    )
    return out.reshape(2, angles, AL)


def complex_add(left, right):
    if left is None or right is None:
        return right if left is None else left
    return left[0] + right[0], left[1] + right[1]


def complex_sub(left, right):
    if right is None:
        return left
    if left is None:
        return -right[0], -right[1]
    return left[0] - right[0], left[1] - right[1]


def rotated(value, turn, size):
    if value is None:
        return None
    real, imag = value
    turn = turn % size
    if turn == 0:
        return value
    if 4 * turn == size:
        return imag, -real
    if 2 * turn == size:
        return -real, -imag
    if 4 * turn == 3 * size:
        return -imag, real
    cos = math.cos(2.0 * math.pi * turn / size)
    sin = math.sin(2.0 * math.pi * turn / size)
    return real * cos + imag * sin, imag * cos - real * sin


def fourier(values):
    size = len(values)
    if size == 1:
        return values
    even = fourier(values[0::2])
    odd = fourier(values[1::2])
    odd = [rotated(value, turn, size) for turn, value in enumerate(odd)]
    return [complex_add(a, b) for a, b in zip(even, odd)] + [
        complex_sub(a, b) for a, b in zip(even, odd)
    ]


def iota(shape, dim):
    return lax.broadcasted_iota(jnp.int32, shape, dim)


def far_field_kernel(slabs, groups, near, phase, out, *scratch):
    (
        plain, code, both, lens, prop, field, band_cos, band_sin, vert, sums, cols, got, mid,
        turned, twiddle, coarse_table, local_sem, send_sem, recv_sem, col_send, col_recv,
    ) = scratch
    steps, lat_dev, width = phase.shape
    _, rows, points = both.shape
    devices = slabs * groups
    angles = AV // devices
    total_rows = lat_dev * slabs
    modulus = 2 * total_rows
    fine = modulus // rows
    band = band_cos.shape[1]
    slab = lax.axis_index("slab")
    grp = lax.axis_index("grp")
    me = slab * groups + grp
    peers = range(1, groups)

    barrier = pltpu.get_barrier_semaphore()

    def greet(step, carry):
        peer = me ^ step
        pl.semaphore_signal(
            barrier,
            inc=1,
            device_id=(lax.div(peer, groups), lax.rem(peer, groups)),
            device_id_type=pl.DeviceIdType.MESH,
        )
        return carry

    lax.fori_loop(1, devices, greet, 0)

    def rows_of(peer):
        return pl.ds(pl.multiple_of(peer * rows, rows), rows)

    def place_of(peer):
        return pl.ds(pl.multiple_of(peer * width, width), width)

    load_phase = [
        pltpu.make_async_copy(phase.at[k], plain.at[k], local_sem.at[k]) for k in range(steps)
    ]
    for copy in load_phase:
        copy.start()
    own_field = pltpu.make_async_copy(
        near.at[:, rows_of(grp)], both.at[:, :, place_of(grp)], local_sem.at[steps]
    )
    own_field.start()
    pl.semaphore_wait(barrier, devices - 1)

    def remote(source, target, slot, step):
        return pltpu.make_async_remote_copy(
            src_ref=source,
            dst_ref=target,
            send_sem=send_sem.at[slot, step],
            recv_sem=recv_sem.at[slot, step],
            device_id=(slab, grp ^ step),
            device_id_type=pl.DeviceIdType.MESH,
        )

    send_field = {
        step: remote(near.at[:, rows_of(grp ^ step)], both.at[:, :, place_of(grp)], steps, step)
        for step in peers
    }
    send_lens = [
        {
            step: remote(
                code.at[k, rows_of(grp ^ step)], lens.at[k, :, place_of(grp)], k, step
            )
            for step in peers
        }
        for k in range(steps)
    ]
    for step in reversed(peers):
        send_field[step].start()

    own_lens = []
    for k in range(steps):
        load_phase[k].wait()

        def encode(index, carry):
            part = pl.ds(pl.multiple_of(index * 32, 32), 32)
            code[k, part] = jnp.exp(plain[k, part] * (PHASE_CODE * math.log(2.0))).astype(
                jnp.bfloat16
            )
            return carry

        lax.fori_loop(0, lat_dev // 32, encode, 0)
        own_lens.append(
            pltpu.make_async_copy(
                code.at[k, rows_of(grp)], lens.at[k, :, place_of(grp)], local_sem.at[k]
            )
        )
        own_lens[k].start()

    gain = 1.0 / math.sqrt(points)
    tall = 32

    def make_band(index, carry):
        start = pl.multiple_of(index * tall, tall)
        offset = iota((tall, band), 1) - iota((tall, band), 0) - start
        cos, sin = unit_angle(offset * offset - points // 4, 2 * points)
        for ref, value in ((band_cos, cos), (band_sin, sin)):
            value = (value * gain).astype(jnp.bfloat16)
            ref[pl.ds(start, tall)] = value
            ref[pl.ds(start + points, tall)] = value
        return carry

    lax.fori_loop(0, points // tall, make_band, 0)

    def make_vert(index, carry):
        start = pl.multiple_of(index * 16, 16)
        for left in range(0, points, 512):
            shape = (16, min(512, points))
            angle = iota(shape, 0) + (start - AV // 2)
            point = iota(shape, 1) + (left - points // 2)
            cos, sin = unit_angle(angle * point, 2 * points)
            part = pl.ds(left, shape[1])
            vert[pl.ds(start, 16), part] = cos.astype(jnp.bfloat16)
            vert[pl.ds(start + AV, 16), part] = sin.astype(jnp.bfloat16)
        return carry

    lax.fori_loop(0, AV // 16, make_vert, 0)

    shape = (fine, rows)
    number = iota(shape, 0)
    cos, sin = unit_angle(number * iota(shape, 1) - number * (total_rows // 2), modulus)
    scale = 1.0 / math.sqrt(total_rows * points)
    twiddle[0] = cos * scale
    twiddle[1] = sin * scale
    coarse = AL // fine
    half = coarse // 2
    shape = (half, rows)
    for parity in range(2):
        number = 2 * iota(shape, 0) + parity
        cos, sin = unit_angle(iota(shape, 1) * (number * fine - AL // 2), modulus)
        cos = cos.astype(jnp.bfloat16)
        sin = sin.astype(jnp.bfloat16)
        top = parity * coarse
        coarse_table[top : top + half, :rows] = cos
        coarse_table[top : top + half, rows:] = sin
        coarse_table[top + half : top + coarse, :rows] = -sin
        coarse_table[top + half : top + coarse, rows:] = cos

    def propagate(source):
        def block(index, carry):
            start = pl.multiple_of(lax.rem(points - index * band, points), band)
            part = pl.ds(pl.multiple_of(index * band, band), band)
            left = source()
            with_cos = matmul(left, band_cos[pl.ds(start, points)])
            with_sin = matmul(left, band_sin[pl.ds(start, points)])
            prop[0, :, part] = (with_cos[:rows] - with_sin[rows:]).astype(jnp.bfloat16)
            prop[1, :, part] = (with_sin[:rows] + with_cos[rows:]).astype(jnp.bfloat16)
            return carry

        lax.fori_loop(0, points // band, block, 0)

    def focus(k, peer):
        left = pl.multiple_of(peer * width, width)

        def part_of(index, carry):
            start = pl.multiple_of(index * 16, 16)
            part = pl.ds(left, width)
            real = prop[0, pl.ds(start, 16), part].astype(jnp.float32)
            imag = prop[1, pl.ds(start, 16), part].astype(jnp.float32)
            angle = jnp.log(lens[k, pl.ds(start, 16), part].astype(jnp.float32)) * (
                1.0 / (PHASE_CODE * math.log(2.0))
            )
            cos, sin = sincos(angle)
            field[pl.ds(start, 16), part] = (real * cos - imag * sin).astype(jnp.bfloat16)
            field[pl.ds(start + rows, 16), part] = (real * sin + imag * cos).astype(jnp.bfloat16)
            return carry

        lax.fori_loop(0, rows // 16, part_of, 0)

    for step in peers:
        send_field[step].wait_send()
    for step in reversed(peers):
        send_lens[0][step].start()
    own_field.wait()
    for step in peers:
        send_field[step].wait_recv()
    propagate(lambda: both[...].reshape(2 * rows, points))
    for k in range(1, steps):
        for step in peers:
            send_lens[k - 1][step].wait_send()
        for step in reversed(peers):
            send_lens[k][step].start()
        own_lens[k - 1].wait()
        focus(k - 1, grp)
        for step in peers:
            send_lens[k - 1][step].wait_recv()
            focus(k - 1, grp ^ step)
        propagate(lambda: field[...])

    for step in range(groups):
        if step == 0:
            own_lens[steps - 1].wait()
        else:
            send_lens[steps - 1][step].wait_recv()
        peer = grp ^ step
        focus(steps - 1, peer)
        term = lax.dot_general(
            vert[:, place_of(peer)],
            field[:, place_of(peer)],
            (((1,), (1,)), ((), ())),
            preferred_element_type=jnp.float32,
        )
        if step == 0:
            sums[...] = term
        elif step < groups - 1:
            sums[...] += term
        else:
            term = sums[...] + term
            cols[0] = (term[:AV, :rows] + term[AV:, rows:]).astype(jnp.bfloat16)
            cols[1] = (term[:AV, rows:] - term[AV:, :rows]).astype(jnp.bfloat16)

    def part_for(peer):
        return cols.at[:, pl.ds(pl.multiple_of(peer * angles, angles), angles)]

    def column_copy(step):
        peer = me ^ step
        return pltpu.make_async_remote_copy(
            src_ref=part_for(peer),
            dst_ref=got.at[me],
            send_sem=col_send.at[step],
            recv_sem=col_recv.at[step],
            device_id=(lax.div(peer, groups), lax.rem(peer, groups)),
            device_id_type=pl.DeviceIdType.MESH,
        )

    own_cols = pltpu.make_async_copy(part_for(me), got.at[me], local_sem.at[0])
    for across in reversed(range(groups)):

        def send(index, carry):
            column_copy(index * groups + across).start()
            return carry

        lax.fori_loop(1 if across == 0 else 0, slabs, send, 0)
    own_cols.start()
    for step in peers:
        send_lens[steps - 1][step].wait_send()
    own_cols.wait()

    def receive(step, carry):
        column_copy(step).wait_recv()
        return carry

    lax.fori_loop(1, devices, receive, 0)

    inner = 8
    outer = fine // inner
    for low in range(outer):
        values = []
        for high in range(inner):
            source = high * outer + low
            if source < devices:
                values.append(
                    (got[source, 0].astype(jnp.float32), got[source, 1].astype(jnp.float32))
                )
            else:
                values.append(None)
        for turn, value in enumerate(fourier(values)):
            real, imag = rotated(value, low * turn, fine)
            mid[low * inner + turn, 0] = real
            mid[low * inner + turn, 1] = imag
    for turn in range(inner):
        values = [
            (mid[low * inner + turn, 0], mid[low * inner + turn, 1]) for low in range(outer)
        ]
        for high, (real, imag) in enumerate(fourier(values)):
            number = high * inner + turn
            cos = twiddle[0, number : number + 1]
            sin = twiddle[1, number : number + 1]
            turned[0, pl.ds(number, angles, stride=fine)] = real * cos + imag * sin
            turned[1, pl.ds(number, angles, stride=fine)] = imag * cos - real * sin
    lanes = 2 * fine
    low_half = iota((coarse, lanes), 1) < fine
    table = coarse_table[...]
    for pair in range(angles // 2):
        part = pl.ds(pair * lanes, lanes)
        right = jnp.concatenate(
            [turned[0, part].astype(jnp.bfloat16), turned[1, part].astype(jnp.bfloat16)], axis=1
        )
        result = lax.dot_general(
            table, right, (((1,), (1,)), ((), ())), preferred_element_type=jnp.float32
        )
        even = result[:coarse]
        odd = result[coarse:]
        first = jnp.where(low_half, even, pltpu.roll(odd, fine, 1))
        second = jnp.where(low_half, pltpu.roll(even, fine, 1), odd)
        for c in range(2):
            out[c, 2 * pair] = first[c * half : (c + 1) * half]
            out[c, 2 * pair + 1] = second[c * half : (c + 1) * half]

    def sent(step, carry):
        column_copy(step).wait_send()
        return carry

    lax.fori_loop(1, devices, sent, 0)


def one_kernel(near_field, lens_phase):
    slabs = lax.axis_size("slab")
    groups = lax.axis_size("grp")
    devices = slabs * groups
    steps, lat_dev, width = lens_phase.shape
    points = width * groups
    rows = lat_dev // groups
    angles = AV // devices
    fine = 2 * lat_dev * slabs // rows
    coarse = AL // fine
    band = math.gcd(points, 256)
    bf16 = jnp.bfloat16

    def kernel(*refs):
        far_field_kernel(slabs, groups, *refs)

    out = pl.pallas_call(
        kernel,
        out_shape=jax.ShapeDtypeStruct((2, angles, coarse // 2, 2 * fine), jnp.float32),
        in_specs=[pl.BlockSpec(memory_space=pl.ANY)] * 2,
        out_specs=pl.BlockSpec(memory_space=pltpu.VMEM),
        scratch_shapes=[
            pltpu.VMEM(lens_phase.shape, jnp.float32),
            pltpu.VMEM(lens_phase.shape, bf16),
            pltpu.VMEM((2, rows, points), bf16),
            pltpu.VMEM((steps, rows, points), bf16),
            pltpu.VMEM((2, rows, points), bf16),
            pltpu.VMEM((2 * rows, points), bf16),
            pltpu.VMEM((2 * points, band), bf16),
            pltpu.VMEM((2 * points, band), bf16),
            pltpu.VMEM((2 * AV, points), bf16),
            pltpu.VMEM((2 * AV, 2 * rows), jnp.float32),
            pltpu.VMEM((2, AV, rows), bf16),
            pltpu.VMEM((devices, 2, angles, rows), bf16),
            pltpu.VMEM((fine, 2, angles, rows), jnp.float32),
            pltpu.VMEM((2, angles * fine, rows), jnp.float32),
            pltpu.VMEM((2, fine, rows), jnp.float32),
            pltpu.VMEM((2 * coarse, 2 * rows), bf16),
            pltpu.SemaphoreType.DMA((steps + 1,)),
            pltpu.SemaphoreType.DMA((steps + 1, groups)),
            pltpu.SemaphoreType.DMA((steps + 1, groups)),
            pltpu.SemaphoreType.DMA((devices,)),
            pltpu.SemaphoreType.DMA((devices,)),
        ],
        compiler_params=pltpu.CompilerParams(
            collective_id=1, has_side_effects=True, vmem_limit_bytes=48 * 1024 * 1024
        ),
        name="far_field",
    )(near_field, lens_phase)
    return out.reshape(2, angles, AL)


def fits_one_kernel(mesh, shape):
    slabs = mesh.shape["slab"]
    groups = mesh.shape["grp"]
    devices = slabs * groups
    _, total_rows, points = shape
    rows = total_rows // devices
    powers = all(size & (size - 1) == 0 for size in (slabs, groups, points, total_rows))
    return powers and rows == 128 and AV // devices == 16 and 2 * total_rows // rows == 64


def solution(mesh):
    spec = P(None, "slab", "grp")

    def far_field(near_field, lens_phase):
        body = one_kernel if fits_one_kernel(mesh, lens_phase.shape) else on_device
        return jax.shard_map(
            body,
            mesh=mesh,
            in_specs=(spec, spec),
            out_specs=P(None, ("slab", "grp"), None),
            check_vma=False,
        )(near_field, lens_phase)

    return far_field
```

```python
import math

import jax
import jax.numpy as jnp
from jax import lax
from jax.experimental import pallas as pl
from jax.experimental.pallas import tpu as pltpu
from jax.sharding import PartitionSpec as P

AV = 512
AL = 2048
PHASE_CODE = 40.0


def sincos(angle):
    half = 0.5 * angle
    sq = half * half
    sin = -1.0 / 39916800.0
    for term in (1.0 / 362880.0, -1.0 / 5040.0, 1.0 / 120.0, -1.0 / 6.0, 1.0):
        sin = sin * sq + term
    sin = sin * half
    cos = 1.0 / 479001600.0
    for term in (-1.0 / 3628800.0, 1.0 / 40320.0, -1.0 / 720.0, 1.0 / 24.0, -0.5, 1.0):
        cos = cos * sq + term
    return 1.0 - 2.0 * sin * sin, 2.0 * sin * cos


def unit_angle(turns, modulus):
    assert modulus & (modulus - 1) == 0
    centred = ((turns + modulus // 2) & (modulus - 1)) - modulus // 2
    return sincos(centred.astype(jnp.float32) * (2.0 * math.pi / modulus))


def count(size):
    return lax.optimization_barrier(jnp.arange(size, dtype=jnp.int32))


def phase_table(row_index, col_index, modulus):
    cos, sin = unit_angle(row_index[:, None] * col_index[None, :], modulus)
    return cos.astype(jnp.bfloat16), sin.astype(jnp.bfloat16)


def conjugate(table):
    cos, sin = table
    return jnp.stack([jnp.stack([cos, -sin]), jnp.stack([sin, cos])])


def propagator(points):
    band = math.gcd(points, 256)
    offset = count(points)[None, :] - count(band)[:, None]
    cos, sin = unit_angle(offset * offset - points // 4, 2 * points)
    gain = 1.0 / math.sqrt(points)

    def rolled(part):
        part = lax.optimization_barrier((part * gain).astype(jnp.bfloat16))
        twice = jnp.concatenate([part, part], axis=1)
        return jnp.concatenate(
            [
                lax.slice_in_dim(twice, points - start, 2 * points - start, axis=1)
                for start in range(0, points, band)
            ]
        )

    return rolled(cos), rolled(sin)


def matmul(left, right):
    return jnp.dot(left, right, preferred_element_type=jnp.float32)


def complex_product(both, table_cos, table_sin):
    rows = both.shape[0] // 2
    with_cos = matmul(both, table_cos)
    with_sin = matmul(both, table_sin)
    return with_cos[:rows] - with_sin[rows:], with_sin[:rows] + with_cos[rows:]


def exchange_kernel(groups, devices, source, target, send_sem, recv_sem, own_sem):
    me = lax.axis_index("slab") * groups + lax.axis_index("grp")
    barrier = pltpu.get_barrier_semaphore()

    def place(device):
        return (lax.div(device, groups), lax.rem(device, groups))

    def greet(step, carry):
        peer = lax.rem(me + step, devices)
        pl.semaphore_signal(
            barrier, inc=1, device_id=place(peer), device_id_type=pl.DeviceIdType.MESH
        )
        return carry

    lax.fori_loop(1, devices, greet, 0)
    pl.semaphore_wait(barrier, devices - 1)

    def block(step):
        peer = lax.rem(me + step, devices)
        return pltpu.make_async_remote_copy(
            src_ref=source.at[peer],
            dst_ref=target.at[me],
            send_sem=send_sem.at[step],
            recv_sem=recv_sem.at[step],
            device_id=place(peer),
            device_id_type=pl.DeviceIdType.MESH,
        )

    def send(step, carry):
        block(step).start()
        return carry

    def wait(step, carry):
        block(step).wait()
        return carry

    lax.fori_loop(1, devices, send, 0)
    own = pltpu.make_async_copy(source.at[me], target.at[me], own_sem)
    own.start()
    own.wait()
    lax.fori_loop(1, devices, wait, 0)


def exchange(blocks, groups):
    devices = blocks.shape[0]

    def kernel(*refs):
        exchange_kernel(groups, devices, *refs)

    return pl.pallas_call(
        kernel,
        out_shape=jax.ShapeDtypeStruct(blocks.shape, blocks.dtype),
        in_specs=[pl.BlockSpec(memory_space=pltpu.VMEM)],
        out_specs=pl.BlockSpec(memory_space=pltpu.VMEM),
        scratch_shapes=[
            pltpu.SemaphoreType.DMA((devices,)),
            pltpu.SemaphoreType.DMA((devices,)),
            pltpu.SemaphoreType.DMA,
        ],
        compiler_params=pltpu.CompilerParams(collective_id=0, has_side_effects=True),
        name="column_exchange",
    )(blocks)


def on_device(near_field, lens_phase):
    slab_count = lax.axis_size("slab")
    group_count = lax.axis_size("grp")
    devices = slab_count * group_count
    steps, lat_dev, width = lens_phase.shape
    points = width * group_count
    total_rows = lat_dev * slab_count
    rows = lat_dev // group_count
    angles = AV // devices
    coded = [jnp.exp2(lens_phase[k] * PHASE_CODE).astype(jnp.bfloat16) for k in range(steps)]
    blocks = jnp.transpose(near_field.reshape(2, group_count, rows, width), (1, 0, 2, 3))
    field = lax.all_to_all(blocks, "grp", split_axis=0, concat_axis=0, tiled=True)
    arrived = field
    moved = []
    for part in coded:
        part, arrived = lax.optimization_barrier((part, arrived))
        if not moved:
            field = arrived
        else:
            moved[-1] = arrived
        arrived = lax.all_to_all(part, "grp", split_axis=0, concat_axis=1, tiled=True)
        moved.append(arrived)
    coded = moved
    prop_cos, prop_sin = propagator(points)
    both = jnp.transpose(field, (1, 2, 0, 3)).reshape(2 * rows, points)
    for section in range(steps):
        real, imag = complex_product(both, prop_cos, prop_sin)
        real = real.astype(jnp.bfloat16).astype(jnp.float32)
        imag = imag.astype(jnp.bfloat16).astype(jnp.float32)
        phase = jnp.log2(coded[section].astype(jnp.float32)) * (1.0 / PHASE_CODE)
        lens_cos, lens_sin = sincos(phase)
        both = jnp.concatenate(
            [
                (real * lens_cos - imag * lens_sin).astype(jnp.bfloat16),
                (real * lens_sin + imag * lens_cos).astype(jnp.bfloat16),
            ]
        )
    vert_cos, vert_sin = phase_table(
        count(AV) - AV // 2, count(points) - points // 2, 2 * points
    )
    vert_cos, vert_sin = lax.optimization_barrier((vert_cos, vert_sin))
    with_cos = jnp.einsum("av,nv->an", vert_cos, both, preferred_element_type=jnp.float32)
    with_sin = jnp.einsum("av,nv->an", vert_sin, both, preferred_element_type=jnp.float32)
    col_real = (with_cos[:, :rows] + with_sin[:, rows:]).astype(jnp.bfloat16)
    col_imag = (with_cos[:, rows:] - with_sin[:, :rows]).astype(jnp.bfloat16)
    cols = jnp.stack([part.reshape(devices, angles, rows) for part in (col_real, col_imag)], axis=1)
    got = exchange(cols.reshape(devices, 2 * angles, rows), group_count)
    modulus = 2 * total_rows
    period = modulus // rows
    source = count(devices) - devices // 2
    fine = count(period)
    near = count(rows)
    coarse = count(AL // period)
    scale = 1.0 / math.sqrt(total_rows * points)
    got = got.reshape(devices, 2, angles, rows)
    weights = conjugate(phase_table(source, fine, period))
    mid = jnp.einsum("skam,kcsf->cafm", got, weights, preferred_element_type=jnp.float32)
    t_cos, t_sin = unit_angle(fine[:, None] * near[None, :], modulus)
    t_cos = t_cos * scale
    t_sin = t_sin * scale
    turned = jnp.stack([mid[0] * t_cos + mid[1] * t_sin, mid[1] * t_cos - mid[0] * t_sin])
    weights = conjugate(phase_table(near, coarse * period - AL // 2, modulus))
    out = jnp.einsum(
        "kafm,kcmd->cadf", turned.astype(jnp.bfloat16), weights, preferred_element_type=jnp.float32
    )
    return out.reshape(2, angles, AL)


def complex_add(left, right):
    if left is None or right is None:
        return right if left is None else left
    return left[0] + right[0], left[1] + right[1]


def complex_sub(left, right):
    if right is None:
        return left
    if left is None:
        return -right[0], -right[1]
    return left[0] - right[0], left[1] - right[1]


def rotated(value, turn, size):
    if value is None:
        return None
    real, imag = value
    turn = turn % size
    if turn == 0:
        return value
    if 4 * turn == size:
        return imag, -real
    if 2 * turn == size:
        return -real, -imag
    if 4 * turn == 3 * size:
        return -imag, real
    cos = math.cos(2.0 * math.pi * turn / size)
    sin = math.sin(2.0 * math.pi * turn / size)
    return real * cos + imag * sin, imag * cos - real * sin


def fourier(values):
    size = len(values)
    if size == 1:
        return values
    even = fourier(values[0::2])
    odd = fourier(values[1::2])
    odd = [rotated(value, turn, size) for turn, value in enumerate(odd)]
    return [complex_add(a, b) for a, b in zip(even, odd)] + [
        complex_sub(a, b) for a, b in zip(even, odd)
    ]


def iota(shape, dim):
    return lax.broadcasted_iota(jnp.int32, shape, dim)


def far_field_kernel(slabs, groups, near, phase, out, *scratch):
    (
        plain, code, both, lens, prop, field, band_cos, band_sin, vert, sums, cols, got, mid,
        turned, twiddle, coarse_table, local_sem, send_sem, recv_sem, col_send, col_recv,
        met_sem,
    ) = scratch
    steps, lat_dev, width = phase.shape
    _, rows, points = both.shape
    devices = slabs * groups
    angles = AV // devices
    total_rows = lat_dev * slabs
    modulus = 2 * total_rows
    fine = modulus // rows
    band = band_cos.shape[1]
    slab = lax.axis_index("slab")
    grp = lax.axis_index("grp")
    me = slab * groups + grp
    peers = range(1, groups)

    def signal(semaphore, device):
        pl.semaphore_signal(
            semaphore, inc=1, device_id=device, device_id_type=pl.DeviceIdType.MESH
        )

    barrier = pltpu.get_barrier_semaphore()
    bits = slabs.bit_length() - 1
    for step in peers:
        signal(barrier, (slab, grp ^ step))
    for bit in range(bits):
        signal(barrier, (slab ^ (1 << bit), grp))

    def pass_on(bit):
        if bit > 0:
            pl.semaphore_wait(met_sem.at[bit - 1], 1)
        if bit < bits:
            signal(met_sem.at[bit], (slab ^ (1 << bit), grp))

    def rows_of(peer):
        return pl.ds(pl.multiple_of(peer * rows, rows), rows)

    def place_of(peer):
        return pl.ds(pl.multiple_of(peer * width, width), width)

    load_phase = [
        pltpu.make_async_copy(phase.at[k], plain.at[k], local_sem.at[k]) for k in range(steps)
    ]
    for copy in load_phase:
        copy.start()
    own_field = pltpu.make_async_copy(
        near.at[:, rows_of(grp)], both.at[:, :, place_of(grp)], local_sem.at[steps]
    )
    own_field.start()
    pl.semaphore_wait(barrier, groups - 1 + bits)

    def remote(source, target, slot, step):
        return pltpu.make_async_remote_copy(
            src_ref=source,
            dst_ref=target,
            send_sem=send_sem.at[slot, step],
            recv_sem=recv_sem.at[slot, step],
            device_id=(slab, grp ^ step),
            device_id_type=pl.DeviceIdType.MESH,
        )

    send_field = {
        step: remote(near.at[:, rows_of(grp ^ step)], both.at[:, :, place_of(grp)], steps, step)
        for step in peers
    }
    send_lens = [
        {
            step: remote(
                code.at[k, rows_of(grp ^ step)], lens.at[k, :, place_of(grp)], k, step
            )
            for step in peers
        }
        for k in range(steps)
    ]
    for step in reversed(peers):
        send_field[step].start()
    pass_on(0)

    own_lens = []
    for k in range(steps):
        load_phase[k].wait()

        def encode(index, carry):
            part = pl.ds(pl.multiple_of(index * 32, 32), 32)
            code[k, part] = jnp.exp(plain[k, part] * (PHASE_CODE * math.log(2.0))).astype(
                jnp.bfloat16
            )
            return carry

        lax.fori_loop(0, lat_dev // 32, encode, 0)
        own_lens.append(
            pltpu.make_async_copy(
                code.at[k, rows_of(grp)], lens.at[k, :, place_of(grp)], local_sem.at[k]
            )
        )
        own_lens[k].start()

    gain = 1.0 / math.sqrt(points)
    tall = 32

    def make_band(index, carry):
        start = pl.multiple_of(index * tall, tall)
        offset = iota((tall, band), 1) - iota((tall, band), 0) - start
        cos, sin = unit_angle(offset * offset - points // 4, 2 * points)
        for ref, value in ((band_cos, cos), (band_sin, sin)):
            value = (value * gain).astype(jnp.bfloat16)
            ref[pl.ds(start, tall)] = value
            ref[pl.ds(start + points, tall)] = value
        return carry

    lax.fori_loop(0, points // tall, make_band, 0)

    def make_vert(index, carry):
        start = pl.multiple_of(index * 16, 16)
        for left in range(0, points, 512):
            shape = (16, min(512, points))
            angle = iota(shape, 0) + (start - AV // 2)
            point = iota(shape, 1) + (left - points // 2)
            cos, sin = unit_angle(angle * point, 2 * points)
            part = pl.ds(left, shape[1])
            vert[pl.ds(start, 16), part] = cos.astype(jnp.bfloat16)
            vert[pl.ds(start + AV, 16), part] = sin.astype(jnp.bfloat16)
        return carry

    lax.fori_loop(0, AV // 16, make_vert, 0)

    shape = (fine, rows)
    number = iota(shape, 0)
    cos, sin = unit_angle(number * iota(shape, 1) - number * (total_rows // 2), modulus)
    scale = 1.0 / math.sqrt(total_rows * points)
    twiddle[0] = cos * scale
    twiddle[1] = sin * scale
    coarse = AL // fine
    half = coarse // 2
    shape = (half, rows)
    for parity in range(2):
        number = 2 * iota(shape, 0) + parity
        cos, sin = unit_angle(iota(shape, 1) * (number * fine - AL // 2), modulus)
        cos = cos.astype(jnp.bfloat16)
        sin = sin.astype(jnp.bfloat16)
        top = parity * coarse
        coarse_table[top : top + half, :rows] = cos
        coarse_table[top : top + half, rows:] = sin
        coarse_table[top + half : top + coarse, :rows] = -sin
        coarse_table[top + half : top + coarse, rows:] = cos

    def propagate(source):
        def block(index, carry):
            start = pl.multiple_of(lax.rem(points - index * band, points), band)
            part = pl.ds(pl.multiple_of(index * band, band), band)
            left = source()
            with_cos = matmul(left, band_cos[pl.ds(start, points)])
            with_sin = matmul(left, band_sin[pl.ds(start, points)])
            prop[0, :, part] = (with_cos[:rows] - with_sin[rows:]).astype(jnp.bfloat16)
            prop[1, :, part] = (with_sin[:rows] + with_cos[rows:]).astype(jnp.bfloat16)
            return carry

        lax.fori_loop(0, points // band, block, 0)

    def focus(k, peer):
        left = pl.multiple_of(peer * width, width)

        def part_of(index, carry):
            start = pl.multiple_of(index * 16, 16)
            part = pl.ds(left, width)
            real = prop[0, pl.ds(start, 16), part].astype(jnp.float32)
            imag = prop[1, pl.ds(start, 16), part].astype(jnp.float32)
            angle = jnp.log(lens[k, pl.ds(start, 16), part].astype(jnp.float32)) * (
                1.0 / (PHASE_CODE * math.log(2.0))
            )
            cos, sin = sincos(angle)
            field[pl.ds(start, 16), part] = (real * cos - imag * sin).astype(jnp.bfloat16)
            field[pl.ds(start + rows, 16), part] = (real * sin + imag * cos).astype(jnp.bfloat16)
            return carry

        lax.fori_loop(0, rows // 16, part_of, 0)

    for bit in range(bits):
        pass_on(bit + 1)
    for step in peers:
        send_field[step].wait_send()
    for step in reversed(peers):
        send_lens[0][step].start()
    own_field.wait()
    for step in peers:
        send_field[step].wait_recv()
    propagate(lambda: both[...].reshape(2 * rows, points))
    for k in range(1, steps):
        for step in peers:
            send_lens[k - 1][step].wait_send()
        for step in reversed(peers):
            send_lens[k][step].start()
        own_lens[k - 1].wait()
        focus(k - 1, grp)
        for step in peers:
            send_lens[k - 1][step].wait_recv()
            focus(k - 1, grp ^ step)
        propagate(lambda: field[...])

    for step in range(groups):
        if step == 0:
            own_lens[steps - 1].wait()
        else:
            send_lens[steps - 1][step].wait_recv()
        peer = grp ^ step
        focus(steps - 1, peer)
        term = lax.dot_general(
            vert[:, place_of(peer)],
            field[:, place_of(peer)],
            (((1,), (1,)), ((), ())),
            preferred_element_type=jnp.float32,
        )
        if step == 0:
            sums[...] = term
        elif step < groups - 1:
            sums[...] += term
        else:
            term = sums[...] + term
            cols[0] = (term[:AV, :rows] + term[AV:, rows:]).astype(jnp.bfloat16)
            cols[1] = (term[:AV, rows:] - term[AV:, :rows]).astype(jnp.bfloat16)

    def part_for(peer):
        return cols.at[:, pl.ds(pl.multiple_of(peer * angles, angles), angles)]

    def column_copy(step):
        peer = me ^ step
        return pltpu.make_async_remote_copy(
            src_ref=part_for(peer),
            dst_ref=got.at[me],
            send_sem=col_send.at[step],
            recv_sem=col_recv.at[step],
            device_id=(lax.div(peer, groups), lax.rem(peer, groups)),
            device_id_type=pl.DeviceIdType.MESH,
        )

    own_cols = pltpu.make_async_copy(part_for(me), got.at[me], local_sem.at[0])
    for across in reversed(range(groups)):

        def send(index, carry):
            column_copy(index * groups + across).start()
            return carry

        lax.fori_loop(1 if across == 0 else 0, slabs, send, 0)
    own_cols.start()
    for step in peers:
        send_lens[steps - 1][step].wait_send()
    own_cols.wait()

    def receive(step, carry):
        column_copy(step).wait_recv()
        return carry

    lax.fori_loop(1, devices, receive, 0)

    inner = 8
    outer = fine // inner
    for low in range(outer):
        values = []
        for high in range(inner):
            source = high * outer + low
            if source < devices:
                values.append(
                    (got[source, 0].astype(jnp.float32), got[source, 1].astype(jnp.float32))
                )
            else:
                values.append(None)
        for turn, value in enumerate(fourier(values)):
            real, imag = rotated(value, low * turn, fine)
            mid[low * inner + turn, 0] = real
            mid[low * inner + turn, 1] = imag
    for turn in range(inner):
        values = [
            (mid[low * inner + turn, 0], mid[low * inner + turn, 1]) for low in range(outer)
        ]
        for high, (real, imag) in enumerate(fourier(values)):
            number = high * inner + turn
            cos = twiddle[0, number : number + 1]
            sin = twiddle[1, number : number + 1]
            turned[0, pl.ds(number, angles, stride=fine)] = real * cos + imag * sin
            turned[1, pl.ds(number, angles, stride=fine)] = imag * cos - real * sin
    lanes = 2 * fine
    low_half = iota((coarse, lanes), 1) < fine
    table = coarse_table[...]
    for pair in range(angles // 2):
        part = pl.ds(pair * lanes, lanes)
        right = jnp.concatenate(
            [turned[0, part].astype(jnp.bfloat16), turned[1, part].astype(jnp.bfloat16)], axis=1
        )
        result = lax.dot_general(
            table, right, (((1,), (1,)), ((), ())), preferred_element_type=jnp.float32
        )
        even = result[:coarse]
        odd = result[coarse:]
        first = jnp.where(low_half, even, pltpu.roll(odd, fine, 1))
        second = jnp.where(low_half, pltpu.roll(even, fine, 1), odd)
        for c in range(2):
            for angle, value in ((2 * pair, first), (2 * pair + 1, second)):
                row = (c * angles + angle // 8 * 8) * half + angle % 8
                out[pl.ds(row, half, stride=8)] = value[c * half : (c + 1) * half]

    def sent(step, carry):
        column_copy(step).wait_send()
        return carry

    lax.fori_loop(1, devices, sent, 0)


def one_kernel(near_field, lens_phase):
    slabs = lax.axis_size("slab")
    groups = lax.axis_size("grp")
    devices = slabs * groups
    steps, lat_dev, width = lens_phase.shape
    points = width * groups
    rows = lat_dev // groups
    angles = AV // devices
    fine = 2 * lat_dev * slabs // rows
    coarse = AL // fine
    band = math.gcd(points, 256)
    bf16 = jnp.bfloat16

    def kernel(*refs):
        far_field_kernel(slabs, groups, *refs)

    out = pl.pallas_call(
        kernel,
        out_shape=jax.ShapeDtypeStruct((angles * coarse, 2 * fine), jnp.float32),
        in_specs=[pl.BlockSpec(memory_space=pl.ANY)] * 2,
        out_specs=pl.BlockSpec(memory_space=pltpu.VMEM),
        scratch_shapes=[
            pltpu.VMEM(lens_phase.shape, jnp.float32),
            pltpu.VMEM(lens_phase.shape, bf16),
            pltpu.VMEM((2, rows, points), bf16),
            pltpu.VMEM((steps, rows, points), bf16),
            pltpu.VMEM((2, rows, points), bf16),
            pltpu.VMEM((2 * rows, points), bf16),
            pltpu.VMEM((2 * points, band), bf16),
            pltpu.VMEM((2 * points, band), bf16),
            pltpu.VMEM((2 * AV, points), bf16),
            pltpu.VMEM((2 * AV, 2 * rows), jnp.float32),
            pltpu.VMEM((2, AV, rows), bf16),
            pltpu.VMEM((devices, 2, angles, rows), bf16),
            pltpu.VMEM((fine, 2, angles, rows), jnp.float32),
            pltpu.VMEM((2, angles * fine, rows), jnp.float32),
            pltpu.VMEM((2, fine, rows), jnp.float32),
            pltpu.VMEM((2 * coarse, 2 * rows), bf16),
            pltpu.SemaphoreType.DMA((steps + 1,)),
            pltpu.SemaphoreType.DMA((steps + 1, groups)),
            pltpu.SemaphoreType.DMA((steps + 1, groups)),
            pltpu.SemaphoreType.DMA((devices,)),
            pltpu.SemaphoreType.DMA((devices,)),
            pltpu.SemaphoreType.REGULAR((slabs.bit_length(),)),
        ],
        compiler_params=pltpu.CompilerParams(
            collective_id=1, has_side_effects=True, vmem_limit_bytes=53 * 1024 * 1024
        ),
        name="far_field",
    )(near_field, lens_phase)
    out = out.reshape(2, angles // 8, coarse // 2, 8, 2 * fine)
    return jnp.transpose(out, (0, 1, 3, 2, 4)).reshape(2, angles, AL)


def fits_one_kernel(mesh, shape):
    slabs = mesh.shape["slab"]
    groups = mesh.shape["grp"]
    devices = slabs * groups
    _, total_rows, points = shape
    rows = total_rows // devices
    powers = all(size & (size - 1) == 0 for size in (slabs, groups, points, total_rows))
    return powers and rows == 128 and AV // devices == 16 and 2 * total_rows // rows == 64


def solution(mesh):
    spec = P(None, "slab", "grp")

    def far_field(near_field, lens_phase):
        body = one_kernel if fits_one_kernel(mesh, lens_phase.shape) else on_device
        return jax.shard_map(
            body,
            mesh=mesh,
            in_specs=(spec, spec),
            out_specs=P(None, ("slab", "grp"), None),
            check_vma=False,
        )(near_field, lens_phase)

    return far_field
```

```python
import math

import jax
import jax.numpy as jnp
from jax import lax
from jax.experimental import pallas as pl
from jax.experimental.pallas import tpu as pltpu
from jax.sharding import PartitionSpec as P

AV = 512
AL = 2048
PHASE_CODE = 40.0


def sincos(angle):
    half = 0.5 * angle
    sq = half * half
    sin = -1.0 / 39916800.0
    for term in (1.0 / 362880.0, -1.0 / 5040.0, 1.0 / 120.0, -1.0 / 6.0, 1.0):
        sin = sin * sq + term
    sin = sin * half
    cos = 1.0 / 479001600.0
    for term in (-1.0 / 3628800.0, 1.0 / 40320.0, -1.0 / 720.0, 1.0 / 24.0, -0.5, 1.0):
        cos = cos * sq + term
    return 1.0 - 2.0 * sin * sin, 2.0 * sin * cos


def unit_angle(turns, modulus):
    assert modulus & (modulus - 1) == 0
    centred = ((turns + modulus // 2) & (modulus - 1)) - modulus // 2
    return sincos(centred.astype(jnp.float32) * (2.0 * math.pi / modulus))


def count(size):
    return lax.optimization_barrier(jnp.arange(size, dtype=jnp.int32))


def phase_table(row_index, col_index, modulus):
    cos, sin = unit_angle(row_index[:, None] * col_index[None, :], modulus)
    return cos.astype(jnp.bfloat16), sin.astype(jnp.bfloat16)


def conjugate(table):
    cos, sin = table
    return jnp.stack([jnp.stack([cos, -sin]), jnp.stack([sin, cos])])


def propagator(points):
    band = math.gcd(points, 256)
    offset = count(points)[None, :] - count(band)[:, None]
    cos, sin = unit_angle(offset * offset - points // 4, 2 * points)
    gain = 1.0 / math.sqrt(points)

    def rolled(part):
        part = lax.optimization_barrier((part * gain).astype(jnp.bfloat16))
        twice = jnp.concatenate([part, part], axis=1)
        return jnp.concatenate(
            [
                lax.slice_in_dim(twice, points - start, 2 * points - start, axis=1)
                for start in range(0, points, band)
            ]
        )

    return rolled(cos), rolled(sin)


def matmul(left, right):
    return jnp.dot(left, right, preferred_element_type=jnp.float32)


def complex_product(both, table_cos, table_sin):
    rows = both.shape[0] // 2
    with_cos = matmul(both, table_cos)
    with_sin = matmul(both, table_sin)
    return with_cos[:rows] - with_sin[rows:], with_sin[:rows] + with_cos[rows:]


def exchange_kernel(groups, devices, source, target, send_sem, recv_sem, own_sem):
    me = lax.axis_index("slab") * groups + lax.axis_index("grp")
    barrier = pltpu.get_barrier_semaphore()

    def place(device):
        return (lax.div(device, groups), lax.rem(device, groups))

    def greet(step, carry):
        peer = lax.rem(me + step, devices)
        pl.semaphore_signal(
            barrier, inc=1, device_id=place(peer), device_id_type=pl.DeviceIdType.MESH
        )
        return carry

    lax.fori_loop(1, devices, greet, 0)
    pl.semaphore_wait(barrier, devices - 1)

    def block(step):
        peer = lax.rem(me + step, devices)
        return pltpu.make_async_remote_copy(
            src_ref=source.at[peer],
            dst_ref=target.at[me],
            send_sem=send_sem.at[step],
            recv_sem=recv_sem.at[step],
            device_id=place(peer),
            device_id_type=pl.DeviceIdType.MESH,
        )

    def send(step, carry):
        block(step).start()
        return carry

    def wait(step, carry):
        block(step).wait()
        return carry

    lax.fori_loop(1, devices, send, 0)
    own = pltpu.make_async_copy(source.at[me], target.at[me], own_sem)
    own.start()
    own.wait()
    lax.fori_loop(1, devices, wait, 0)


def exchange(blocks, groups):
    devices = blocks.shape[0]

    def kernel(*refs):
        exchange_kernel(groups, devices, *refs)

    return pl.pallas_call(
        kernel,
        out_shape=jax.ShapeDtypeStruct(blocks.shape, blocks.dtype),
        in_specs=[pl.BlockSpec(memory_space=pltpu.VMEM)],
        out_specs=pl.BlockSpec(memory_space=pltpu.VMEM),
        scratch_shapes=[
            pltpu.SemaphoreType.DMA((devices,)),
            pltpu.SemaphoreType.DMA((devices,)),
            pltpu.SemaphoreType.DMA,
        ],
        compiler_params=pltpu.CompilerParams(collective_id=0, has_side_effects=True),
        name="column_exchange",
    )(blocks)


def on_device(near_field, lens_phase):
    slab_count = lax.axis_size("slab")
    group_count = lax.axis_size("grp")
    devices = slab_count * group_count
    steps, lat_dev, width = lens_phase.shape
    points = width * group_count
    total_rows = lat_dev * slab_count
    rows = lat_dev // group_count
    angles = AV // devices
    coded = [jnp.exp2(lens_phase[k] * PHASE_CODE).astype(jnp.bfloat16) for k in range(steps)]
    blocks = jnp.transpose(near_field.reshape(2, group_count, rows, width), (1, 0, 2, 3))
    field = lax.all_to_all(blocks, "grp", split_axis=0, concat_axis=0, tiled=True)
    arrived = field
    moved = []
    for part in coded:
        part, arrived = lax.optimization_barrier((part, arrived))
        if not moved:
            field = arrived
        else:
            moved[-1] = arrived
        arrived = lax.all_to_all(part, "grp", split_axis=0, concat_axis=1, tiled=True)
        moved.append(arrived)
    coded = moved
    prop_cos, prop_sin = propagator(points)
    both = jnp.transpose(field, (1, 2, 0, 3)).reshape(2 * rows, points)
    for section in range(steps):
        real, imag = complex_product(both, prop_cos, prop_sin)
        real = real.astype(jnp.bfloat16).astype(jnp.float32)
        imag = imag.astype(jnp.bfloat16).astype(jnp.float32)
        phase = jnp.log2(coded[section].astype(jnp.float32)) * (1.0 / PHASE_CODE)
        lens_cos, lens_sin = sincos(phase)
        both = jnp.concatenate(
            [
                (real * lens_cos - imag * lens_sin).astype(jnp.bfloat16),
                (real * lens_sin + imag * lens_cos).astype(jnp.bfloat16),
            ]
        )
    vert_cos, vert_sin = phase_table(
        count(AV) - AV // 2, count(points) - points // 2, 2 * points
    )
    vert_cos, vert_sin = lax.optimization_barrier((vert_cos, vert_sin))
    with_cos = jnp.einsum("av,nv->an", vert_cos, both, preferred_element_type=jnp.float32)
    with_sin = jnp.einsum("av,nv->an", vert_sin, both, preferred_element_type=jnp.float32)
    col_real = (with_cos[:, :rows] + with_sin[:, rows:]).astype(jnp.bfloat16)
    col_imag = (with_cos[:, rows:] - with_sin[:, :rows]).astype(jnp.bfloat16)
    cols = jnp.stack([part.reshape(devices, angles, rows) for part in (col_real, col_imag)], axis=1)
    got = exchange(cols.reshape(devices, 2 * angles, rows), group_count)
    modulus = 2 * total_rows
    period = modulus // rows
    source = count(devices) - devices // 2
    fine = count(period)
    near = count(rows)
    coarse = count(AL // period)
    scale = 1.0 / math.sqrt(total_rows * points)
    got = got.reshape(devices, 2, angles, rows)
    weights = conjugate(phase_table(source, fine, period))
    mid = jnp.einsum("skam,kcsf->cafm", got, weights, preferred_element_type=jnp.float32)
    t_cos, t_sin = unit_angle(fine[:, None] * near[None, :], modulus)
    t_cos = t_cos * scale
    t_sin = t_sin * scale
    turned = jnp.stack([mid[0] * t_cos + mid[1] * t_sin, mid[1] * t_cos - mid[0] * t_sin])
    weights = conjugate(phase_table(near, coarse * period - AL // 2, modulus))
    out = jnp.einsum(
        "kafm,kcmd->cadf", turned.astype(jnp.bfloat16), weights, preferred_element_type=jnp.float32
    )
    return out.reshape(2, angles, AL)


SIN_HALF = (9.99999977e-01, -1.66666476e-01, 8.33289957e-03, -1.98008819e-04, 2.59045627e-06)
COS_HALF = (9.99999953e-01, -4.99999053e-01, 4.16635829e-02, -1.38536904e-03, 2.31536098e-05)


def cos_sin(value, scale):
    square = value * value

    def series(terms, start):
        terms = [
            math.sqrt(2.0) * term * (0.5 * scale) ** (2 * power + start)
            for power, term in enumerate(terms)
        ]
        total = terms[-1]
        for term in terms[-2::-1]:
            total = total * square + term
        return total

    sin = series(SIN_HALF, 1) * value
    cos = series(COS_HALF, 0)
    return 1.0 - sin * sin, sin * cos


def table_angle(turns, modulus):
    centred = ((turns + modulus // 2) & (modulus - 1)) - modulus // 2
    return cos_sin(centred.astype(jnp.float32), 2.0 * math.pi / modulus)


def complex_add(left, right):
    if left is None or right is None:
        return right if left is None else left
    return left[0] + right[0], left[1] + right[1]


def complex_sub(left, right):
    if right is None:
        return left
    if left is None:
        return -right[0], -right[1]
    return left[0] - right[0], left[1] - right[1]


def rotated(value, turn, size):
    if value is None:
        return None
    real, imag = value
    turn = turn % size
    if turn == 0:
        return value
    if 4 * turn == size:
        return imag, -real
    if 2 * turn == size:
        return -real, -imag
    if 4 * turn == 3 * size:
        return -imag, real
    cos = math.cos(2.0 * math.pi * turn / size)
    sin = math.sin(2.0 * math.pi * turn / size)
    return real * cos + imag * sin, imag * cos - real * sin


def fourier(values):
    size = len(values)
    if size == 1:
        return values
    even = fourier(values[0::2])
    odd = fourier(values[1::2])
    odd = [rotated(value, turn, size) for turn, value in enumerate(odd)]
    return [complex_add(a, b) for a, b in zip(even, odd)] + [
        complex_sub(a, b) for a, b in zip(even, odd)
    ]


def iota(shape, dim):
    return lax.broadcasted_iota(jnp.int32, shape, dim)


def far_field_kernel(slabs, groups, near, phase, out, *scratch):
    (
        plain, code, both, lens, prop, field, halves, bands, vert, sums, cols, got, mid,
        turned, twiddle, between, coarse_table, local_sem, send_sem, recv_sem, col_send, col_recv,
        met_sem,
    ) = scratch
    steps, lat_dev, width = phase.shape
    _, rows, points = prop.shape
    devices = slabs * groups
    angles = AV // devices
    total_rows = lat_dev * slabs
    modulus = 2 * total_rows
    fine = modulus // rows
    band = bands.shape[2] // 2
    slab = lax.axis_index("slab")
    grp = lax.axis_index("grp")
    me = slab * groups + grp
    peers = sorted(range(1, groups), key=lambda step: (2 * step != groups, step))

    def signal(semaphore, device):
        pl.semaphore_signal(
            semaphore, inc=1, device_id=device, device_id_type=pl.DeviceIdType.MESH
        )

    barrier = pltpu.get_barrier_semaphore()
    bits = slabs.bit_length() - 1
    for step in peers:
        signal(barrier, (slab, grp ^ step))
    for bit in range(bits):
        signal(barrier, (slab ^ (1 << bit), grp))

    def pass_on(bit):
        if bit > 0:
            pl.semaphore_wait(met_sem.at[bit - 1], 1)
        if bit < bits:
            signal(met_sem.at[bit], (slab ^ (1 << bit), grp))

    def rows_of(peer):
        return pl.ds(pl.multiple_of(peer * rows, rows), rows)

    def place_of(peer):
        return pl.ds(pl.multiple_of(peer * width, width), width)

    entrance_part = both.at[:, :, place_of(grp)]
    load_phase = [
        pltpu.make_async_copy(phase.at[k], plain.at[k], local_sem.at[k]) for k in range(steps)
    ]
    for copy in load_phase:
        copy.start()
    own_field = pltpu.make_async_copy(
        near.at[:, rows_of(grp)], entrance_part, local_sem.at[steps]
    )
    own_field.start()
    pl.semaphore_wait(barrier, groups - 1 + bits)

    def remote(source, target, slot, step):
        return pltpu.make_async_remote_copy(
            src_ref=source,
            dst_ref=target,
            send_sem=send_sem.at[slot, step],
            recv_sem=recv_sem.at[slot, step],
            device_id=(slab, grp ^ step),
            device_id_type=pl.DeviceIdType.MESH,
        )

    send_field = {
        step: remote(near.at[:, rows_of(grp ^ step)], entrance_part, steps, step)
        for step in peers
    }
    send_lens = [
        {
            step: remote(
                code.at[k, rows_of(grp ^ step)], lens.at[k, :, place_of(grp)], k, step
            )
            for step in peers
        }
        for k in range(steps)
    ]
    for step in peers:
        send_field[step].start()
    pass_on(0)

    own_lens = []
    for k in range(steps):
        load_phase[k].wait()

        def encode(index, carry):
            part = pl.ds(pl.multiple_of(index * 32, 32), 32)
            code[k, part] = jnp.exp(plain[k, part] * (PHASE_CODE * math.log(2.0))).astype(
                jnp.bfloat16
            )
            return carry

        lax.fori_loop(0, lat_dev // 32, encode, 0)
        own_lens.append(
            pltpu.make_async_copy(
                code.at[k, rows_of(grp)], lens.at[k, :, place_of(grp)], local_sem.at[k]
            )
        )
        own_lens[k].start()

    gain = 1.0 / math.sqrt(points)
    tall = 32

    def make_band(index, carry):
        start = pl.multiple_of(index * tall, tall)
        offset = iota((tall, band), 1) - iota((tall, band), 0) - start
        cos, sin = table_angle(offset * offset - points // 4, 2 * points)
        value = jnp.concatenate([cos, sin], axis=1) * gain
        parity = (iota((tall, 2 * band), 0) + iota((tall, 2 * band), 1)) & 1
        for odd in range(2):
            part = jnp.where(parity == odd, value, 0.0).astype(jnp.bfloat16)
            bands[odd, pl.ds(start, tall)] = part
            bands[odd, pl.ds(start + points, tall)] = part
        return carry

    lax.fori_loop(0, points // tall, make_band, 0)

    share = slabs * angles

    def make_vert(device, carry):
        row = lax.rem(device, groups) * (2 * share) + lax.div(device, groups) * angles
        row = pl.multiple_of(row, angles)
        for left in range(0, points, 512):
            shape = (angles, 512)
            angle = iota(shape, 0) + (device * angles - AV // 2)
            point = iota(shape, 1) + (left - points // 2)
            cos, sin = table_angle(angle * point, 2 * points)
            part = pl.ds(left, 512)
            vert[pl.ds(row, angles), part] = cos.astype(jnp.bfloat16)
            vert[pl.ds(pl.multiple_of(row + share, angles), angles), part] = sin.astype(
                jnp.bfloat16
            )
        return carry

    lax.fori_loop(0, devices, make_vert, 0)

    shape = (fine, rows)
    number = iota(shape, 0)
    cos, sin = table_angle(number * iota(shape, 1) - number * (total_rows // 2), modulus)
    scale = 1.0 / math.sqrt(total_rows * points)
    twiddle[0] = cos * scale
    twiddle[1] = sin * scale
    inner = 8
    outer = fine // inner
    shape = (outer * inner, rows)
    number = iota(shape, 0)
    cos, sin = table_angle((number // inner) * (number % inner), fine)
    between[0] = cos
    between[1] = sin
    coarse = AL // fine
    half = coarse // 2
    shape = (half, rows)
    for parity in range(2):
        number = 2 * iota(shape, 0) + parity
        cos, sin = table_angle(iota(shape, 1) * (number * fine - AL // 2), modulus)
        cos = cos.astype(jnp.bfloat16)
        sin = sin.astype(jnp.bfloat16)
        top = parity * coarse
        coarse_table[top : top + half, :rows] = cos
        coarse_table[top : top + half, rows:] = sin
        coarse_table[top + half : top + coarse, :rows] = -sin
        coarse_table[top + half : top + coarse, rows:] = cos

    middle = points // 2

    def propagate(source, between_blocks):
        def halve(index, carry):
            part = pl.ds(pl.multiple_of(index * 16, 16), 16)
            low, high = source(part)
            low = low.astype(jnp.float32)
            high = high.astype(jnp.float32)
            halves[0, part] = (low + high).astype(jnp.bfloat16)
            halves[1, part] = (low - high).astype(jnp.bfloat16)
            return carry

        lax.fori_loop(0, 2 * rows // 16, halve, 0)

        def block(index, carry):
            start = pl.multiple_of(lax.rem(points - index * band, points), band)
            even = matmul(halves[0], bands[0, pl.ds(start, middle)])
            odd = matmul(halves[1], bands[1, pl.ds(start, middle)])
            for upper in range(2):
                term = even - odd if upper else even + odd
                part = pl.ds(pl.multiple_of(index * band + upper * middle, band), band)
                prop[0, :, part] = (term[:rows, :band] - term[rows:, band:]).astype(jnp.bfloat16)
                prop[1, :, part] = (term[:rows, band:] + term[rows:, :band]).astype(jnp.bfloat16)
            return carry

        done = 0
        blocks = middle // band
        for left in range(len(between_blocks), 0, -1):
            stop = max(done, blocks - left)
            lax.fori_loop(done, stop, block, 0)
            done = stop
            between_blocks[-left]()
        lax.fori_loop(done, blocks, block, 0)

    def focus(k, peer):
        left = pl.multiple_of(peer * width, width)

        def part_of(index, carry):
            start = pl.multiple_of(index * 16, 16)
            part = pl.ds(left, width)
            real = prop[0, pl.ds(start, 16), part].astype(jnp.float32)
            imag = prop[1, pl.ds(start, 16), part].astype(jnp.float32)
            power = jnp.log(lens[k, pl.ds(start, 16), part].astype(jnp.float32))
            cos, sin = cos_sin(power, 1.0 / (PHASE_CODE * math.log(2.0)))
            field[pl.ds(start, 16), part] = (real * cos - imag * sin).astype(jnp.bfloat16)
            field[pl.ds(start + rows, 16), part] = (real * sin + imag * cos).astype(jnp.bfloat16)
            return carry

        lax.fori_loop(0, rows // 16, part_of, 0)

    for bit in range(bits):
        pass_on(bit + 1)
    for step in peers:
        send_field[step].wait_send()
        send_lens[0][step].start()
    own_field.wait()
    for step in peers:
        send_field[step].wait_recv()
    entrance = both.reshape(2 * rows, points)

    def follow(k, step):
        def action():
            send_lens[k][step].wait_send()
            send_lens[k + 1][step].start()

        return action

    follows = [[follow(k, step) for step in peers] for k in range(steps - 1)]
    propagate(
        lambda part: (entrance[part, :middle], entrance[part, middle:]),
        [],
    )
    for k in range(1, steps):
        own_lens[k - 1].wait()
        for step in peers:
            send_lens[k - 1][step].wait_recv()
        for step in peers:
            follows[k-1][peers.index(step)]()
        focus(k - 1, grp)
        for step in sorted(peers):
            focus(k - 1, grp ^ step)
        propagate(
            lambda part: (field[part, :middle], field[part, middle:]),
            follows[k] if k < steps - 1 else [],
        )

    def part_for(peer_slab, peer_grp):
        row = (peer_grp * slabs + peer_slab) * angles
        return cols.at[:, pl.ds(pl.multiple_of(row, angles), angles)]

    def column_copy(index, across):
        peer = (slab ^ index, grp ^ across)
        return pltpu.make_async_remote_copy(
            src_ref=part_for(*peer),
            dst_ref=got.at[me],
            send_sem=col_send.at[index, across],
            recv_sem=col_recv.at[index, across],
            device_id=peer,
            device_id_type=pl.DeviceIdType.MESH,
        )

    def over_slabs(across, action):
        def one(index, carry):
            action(column_copy(index, across))
            return carry

        lax.fori_loop(1 if across == 0 else 0, slabs, one, 0)

    def vertical(part, peer):
        return lax.dot_general(
            vert[part, place_of(peer)],
            field[:, place_of(peer)],
            (((1,), (1,)), ((), ())),
            preferred_element_type=jnp.float32,
        )

    own_lens[steps - 1].wait()
    for step in range(groups - 1):
        if step > 0:
            send_lens[steps - 1][step].wait_recv()
        peer = grp ^ step
        focus(steps - 1, peer)
        term = vertical(slice(None), peer)
        sums[...] = term if step == 0 else sums[...] + term
    peer = grp ^ (groups - 1)
    if groups > 1:
        send_lens[steps - 1][groups - 1].wait_recv()
    focus(steps - 1, peer)
    by_distance = sorted(range(groups), key=lambda step: (2 * step != groups, -step))
    for across in by_distance:
        target = grp ^ across
        part = pl.ds(pl.multiple_of(target * (2 * share), 2 * share), 2 * share)
        term = vertical(part, peer)
        if groups > 1:
            term = sums[part] + term
        place = pl.ds(pl.multiple_of(target * share, share), share)
        cols[0, place] = (term[:share, :rows] + term[share:, rows:]).astype(jnp.bfloat16)
        cols[1, place] = (term[:share, rows:] - term[share:, :rows]).astype(jnp.bfloat16)
        over_slabs(across, lambda copy: copy.start())
    own_cols = pltpu.make_async_copy(part_for(slab, grp), got.at[me], local_sem.at[0])
    own_cols.start()
    for step in peers:
        send_lens[steps - 1][step].wait_send()
    own_cols.wait()

    for across in reversed(by_distance):
        over_slabs(across, lambda copy: copy.wait_send())
        over_slabs(across, lambda copy: copy.wait_recv())
        for low_slab in range(outer // groups):
            low = low_slab * groups + (grp ^ across)
            values = [None] * inner
            for high in range(devices // outer):
                source = high * outer + low
                values[high] = (
                    got[source, 0].astype(jnp.float32),
                    got[source, 1].astype(jnp.float32),
                )
            for turn, (real, imag) in enumerate(fourier(values)):
                number = low * inner + turn
                if turn > 0:
                    cos = between[0, pl.ds(number, 1)]
                    sin = between[1, pl.ds(number, 1)]
                    real, imag = real * cos + imag * sin, imag * cos - real * sin
                mid[number, 0] = real
                mid[number, 1] = imag
    for turn in range(inner):
        values = [
            (mid[low * inner + turn, 0], mid[low * inner + turn, 1]) for low in range(outer)
        ]
        for high, (real, imag) in enumerate(fourier(values)):
            number = high * inner + turn
            cos = twiddle[0, number : number + 1]
            sin = twiddle[1, number : number + 1]
            turned[0, pl.ds(number, angles, stride=fine)] = real * cos + imag * sin
            turned[1, pl.ds(number, angles, stride=fine)] = imag * cos - real * sin
    lanes = 2 * fine
    low_half = iota((coarse, lanes), 1) < fine
    table = coarse_table[...]
    for pair in range(angles // 2):
        part = pl.ds(pair * lanes, lanes)
        right = jnp.concatenate(
            [turned[0, part].astype(jnp.bfloat16), turned[1, part].astype(jnp.bfloat16)], axis=1
        )
        result = lax.dot_general(
            table, right, (((1,), (1,)), ((), ())), preferred_element_type=jnp.float32
        )
        even = result[:coarse]
        odd = result[coarse:]
        first = jnp.where(low_half, even, pltpu.roll(odd, fine, 1))
        second = jnp.where(low_half, pltpu.roll(even, fine, 1), odd)
        for c in range(2):
            for angle, value in ((2 * pair, first), (2 * pair + 1, second)):
                row = (c * angles + angle // 8 * 8) * half + angle % 8
                out[pl.ds(row, half, stride=8)] = value[c * half : (c + 1) * half]


def one_kernel(near_field, lens_phase):
    slabs = lax.axis_size("slab")
    groups = lax.axis_size("grp")
    devices = slabs * groups
    steps, lat_dev, width = lens_phase.shape
    points = width * groups
    rows = lat_dev // groups
    angles = AV // devices
    fine = 2 * lat_dev * slabs // rows
    coarse = AL // fine
    band = math.gcd(points, 256)
    bf16 = jnp.bfloat16

    def kernel(*refs):
        far_field_kernel(slabs, groups, *refs)

    out = pl.pallas_call(
        kernel,
        out_shape=jax.ShapeDtypeStruct((angles * coarse, 2 * fine), jnp.float32),
        in_specs=[pl.BlockSpec(memory_space=pl.ANY)] * 2,
        out_specs=pl.BlockSpec(memory_space=pltpu.VMEM),
        scratch_shapes=[
            pltpu.VMEM(lens_phase.shape, jnp.float32),
            pltpu.VMEM(lens_phase.shape, bf16),
            pltpu.VMEM((2, rows, points), bf16),
            pltpu.VMEM((steps, rows, points), bf16),
            pltpu.VMEM((2, rows, points), bf16),
            pltpu.VMEM((2 * rows, points), bf16),
            pltpu.VMEM((2, 2 * rows, points // 2), bf16),
            pltpu.VMEM((2, 2 * points, 2 * band), bf16),
            pltpu.VMEM((2 * AV, points), bf16),
            pltpu.VMEM((2 * AV, 2 * rows), jnp.float32),
            pltpu.VMEM((2, AV, rows), bf16),
            pltpu.VMEM((devices, 2, angles, rows), bf16),
            pltpu.VMEM((fine, 2, angles, rows), jnp.float32),
            pltpu.VMEM((2, angles * fine, rows), jnp.float32),
            pltpu.VMEM((2, fine, rows), jnp.float32),
            pltpu.VMEM((2, fine, rows), jnp.float32),
            pltpu.VMEM((2 * coarse, 2 * rows), bf16),
            pltpu.SemaphoreType.DMA((steps + 1,)),
            pltpu.SemaphoreType.DMA((steps + 1, groups)),
            pltpu.SemaphoreType.DMA((steps + 1, groups)),
            pltpu.SemaphoreType.DMA((slabs, groups)),
            pltpu.SemaphoreType.DMA((slabs, groups)),
            pltpu.SemaphoreType.REGULAR((slabs.bit_length(),)),
        ],
        compiler_params=pltpu.CompilerParams(
            collective_id=1, has_side_effects=True, vmem_limit_bytes=53 * 1024 * 1024
        ),
        name="far_field",
    )(near_field, lens_phase)
    out = out.reshape(2, angles // 8, coarse // 2, 8, 2 * fine)
    return jnp.transpose(out, (0, 1, 3, 2, 4)).reshape(2, angles, AL)


def fits_one_kernel(mesh, shape):
    slabs = mesh.shape["slab"]
    groups = mesh.shape["grp"]
    devices = slabs * groups
    _, total_rows, points = shape
    rows = total_rows // devices
    powers = all(size & (size - 1) == 0 for size in (slabs, groups, points, total_rows))
    return powers and slabs >= 4 and points >= 512 and rows == 128 and AV // devices == 16 and 2 * total_rows // rows == 64


def solution(mesh):
    spec = P(None, "slab", "grp")

    def far_field(near_field, lens_phase):
        body = one_kernel if fits_one_kernel(mesh, lens_phase.shape) else on_device
        return jax.shard_map(
            body,
            mesh=mesh,
            in_specs=(spec, spec),
            out_specs=P(None, ("slab", "grp"), None),
            check_vma=False,
        )(near_field, lens_phase)

    return far_field
```

```python
import math

import jax
import jax.numpy as jnp
from jax import lax
from jax.experimental import pallas as pl
from jax.experimental.pallas import tpu as pltpu
from jax.sharding import PartitionSpec as P

AV = 512
AL = 2048
PHASE_CODE = 40.0


def sincos(angle):
    half = 0.5 * angle
    sq = half * half
    sin = -1.0 / 39916800.0
    for term in (1.0 / 362880.0, -1.0 / 5040.0, 1.0 / 120.0, -1.0 / 6.0, 1.0):
        sin = sin * sq + term
    sin = sin * half
    cos = 1.0 / 479001600.0
    for term in (-1.0 / 3628800.0, 1.0 / 40320.0, -1.0 / 720.0, 1.0 / 24.0, -0.5, 1.0):
        cos = cos * sq + term
    return 1.0 - 2.0 * sin * sin, 2.0 * sin * cos


def unit_angle(turns, modulus):
    assert modulus & (modulus - 1) == 0
    centred = ((turns + modulus // 2) & (modulus - 1)) - modulus // 2
    return sincos(centred.astype(jnp.float32) * (2.0 * math.pi / modulus))


def count(size):
    return lax.optimization_barrier(jnp.arange(size, dtype=jnp.int32))


def phase_table(row_index, col_index, modulus):
    cos, sin = unit_angle(row_index[:, None] * col_index[None, :], modulus)
    return cos.astype(jnp.bfloat16), sin.astype(jnp.bfloat16)


def conjugate(table):
    cos, sin = table
    return jnp.stack([jnp.stack([cos, -sin]), jnp.stack([sin, cos])])


def propagator(points):
    band = math.gcd(points, 256)
    offset = count(points)[None, :] - count(band)[:, None]
    cos, sin = unit_angle(offset * offset - points // 4, 2 * points)
    gain = 1.0 / math.sqrt(points)

    def rolled(part):
        part = lax.optimization_barrier((part * gain).astype(jnp.bfloat16))
        twice = jnp.concatenate([part, part], axis=1)
        return jnp.concatenate(
            [
                lax.slice_in_dim(twice, points - start, 2 * points - start, axis=1)
                for start in range(0, points, band)
            ]
        )

    return rolled(cos), rolled(sin)


def matmul(left, right):
    return jnp.dot(left, right, preferred_element_type=jnp.float32)


def complex_product(both, table_cos, table_sin):
    rows = both.shape[0] // 2
    with_cos = matmul(both, table_cos)
    with_sin = matmul(both, table_sin)
    return with_cos[:rows] - with_sin[rows:], with_sin[:rows] + with_cos[rows:]


def exchange_kernel(groups, devices, source, target, send_sem, recv_sem, own_sem):
    me = lax.axis_index("slab") * groups + lax.axis_index("grp")
    barrier = pltpu.get_barrier_semaphore()

    def place(device):
        return (lax.div(device, groups), lax.rem(device, groups))

    def greet(step, carry):
        peer = lax.rem(me + step, devices)
        pl.semaphore_signal(
            barrier, inc=1, device_id=place(peer), device_id_type=pl.DeviceIdType.MESH
        )
        return carry

    lax.fori_loop(1, devices, greet, 0)
    pl.semaphore_wait(barrier, devices - 1)

    def block(step):
        peer = lax.rem(me + step, devices)
        return pltpu.make_async_remote_copy(
            src_ref=source.at[peer],
            dst_ref=target.at[me],
            send_sem=send_sem.at[step],
            recv_sem=recv_sem.at[step],
            device_id=place(peer),
            device_id_type=pl.DeviceIdType.MESH,
        )

    def send(step, carry):
        block(step).start()
        return carry

    def wait(step, carry):
        block(step).wait()
        return carry

    lax.fori_loop(1, devices, send, 0)
    own = pltpu.make_async_copy(source.at[me], target.at[me], own_sem)
    own.start()
    own.wait()
    lax.fori_loop(1, devices, wait, 0)


def exchange(blocks, groups):
    devices = blocks.shape[0]

    def kernel(*refs):
        exchange_kernel(groups, devices, *refs)

    return pl.pallas_call(
        kernel,
        out_shape=jax.ShapeDtypeStruct(blocks.shape, blocks.dtype),
        in_specs=[pl.BlockSpec(memory_space=pltpu.VMEM)],
        out_specs=pl.BlockSpec(memory_space=pltpu.VMEM),
        scratch_shapes=[
            pltpu.SemaphoreType.DMA((devices,)),
            pltpu.SemaphoreType.DMA((devices,)),
            pltpu.SemaphoreType.DMA,
        ],
        compiler_params=pltpu.CompilerParams(collective_id=0, has_side_effects=True),
        name="column_exchange",
    )(blocks)


def on_device(near_field, lens_phase):
    slab_count = lax.axis_size("slab")
    group_count = lax.axis_size("grp")
    devices = slab_count * group_count
    steps, lat_dev, width = lens_phase.shape
    points = width * group_count
    total_rows = lat_dev * slab_count
    rows = lat_dev // group_count
    angles = AV // devices
    coded = [jnp.exp2(lens_phase[k] * PHASE_CODE).astype(jnp.bfloat16) for k in range(steps)]
    blocks = jnp.transpose(near_field.reshape(2, group_count, rows, width), (1, 0, 2, 3))
    field = lax.all_to_all(blocks, "grp", split_axis=0, concat_axis=0, tiled=True)
    arrived = field
    moved = []
    for part in coded:
        part, arrived = lax.optimization_barrier((part, arrived))
        if not moved:
            field = arrived
        else:
            moved[-1] = arrived
        arrived = lax.all_to_all(part, "grp", split_axis=0, concat_axis=1, tiled=True)
        moved.append(arrived)
    coded = moved
    prop_cos, prop_sin = propagator(points)
    both = jnp.transpose(field, (1, 2, 0, 3)).reshape(2 * rows, points)
    for section in range(steps):
        real, imag = complex_product(both, prop_cos, prop_sin)
        real = real.astype(jnp.bfloat16).astype(jnp.float32)
        imag = imag.astype(jnp.bfloat16).astype(jnp.float32)
        phase = jnp.log2(coded[section].astype(jnp.float32)) * (1.0 / PHASE_CODE)
        lens_cos, lens_sin = sincos(phase)
        both = jnp.concatenate(
            [
                (real * lens_cos - imag * lens_sin).astype(jnp.bfloat16),
                (real * lens_sin + imag * lens_cos).astype(jnp.bfloat16),
            ]
        )
    vert_cos, vert_sin = phase_table(
        count(AV) - AV // 2, count(points) - points // 2, 2 * points
    )
    vert_cos, vert_sin = lax.optimization_barrier((vert_cos, vert_sin))
    with_cos = jnp.einsum("av,nv->an", vert_cos, both, preferred_element_type=jnp.float32)
    with_sin = jnp.einsum("av,nv->an", vert_sin, both, preferred_element_type=jnp.float32)
    col_real = (with_cos[:, :rows] + with_sin[:, rows:]).astype(jnp.bfloat16)
    col_imag = (with_cos[:, rows:] - with_sin[:, :rows]).astype(jnp.bfloat16)
    cols = jnp.stack([part.reshape(devices, angles, rows) for part in (col_real, col_imag)], axis=1)
    got = exchange(cols.reshape(devices, 2 * angles, rows), group_count)
    modulus = 2 * total_rows
    period = modulus // rows
    source = count(devices) - devices // 2
    fine = count(period)
    near = count(rows)
    coarse = count(AL // period)
    scale = 1.0 / math.sqrt(total_rows * points)
    got = got.reshape(devices, 2, angles, rows)
    weights = conjugate(phase_table(source, fine, period))
    mid = jnp.einsum("skam,kcsf->cafm", got, weights, preferred_element_type=jnp.float32)
    t_cos, t_sin = unit_angle(fine[:, None] * near[None, :], modulus)
    t_cos = t_cos * scale
    t_sin = t_sin * scale
    turned = jnp.stack([mid[0] * t_cos + mid[1] * t_sin, mid[1] * t_cos - mid[0] * t_sin])
    weights = conjugate(phase_table(near, coarse * period - AL // 2, modulus))
    out = jnp.einsum(
        "kafm,kcmd->cadf", turned.astype(jnp.bfloat16), weights, preferred_element_type=jnp.float32
    )
    return out.reshape(2, angles, AL)


SIN_HALF = (9.99999977e-01, -1.66666476e-01, 8.33289957e-03, -1.98008819e-04, 2.59045627e-06)
COS_HALF = (9.99999953e-01, -4.99999053e-01, 4.16635829e-02, -1.38536904e-03, 2.31536098e-05)


def cos_sin(value, scale):
    square = value * value

    def series(terms, start):
        terms = [
            math.sqrt(2.0) * term * (0.5 * scale) ** (2 * power + start)
            for power, term in enumerate(terms)
        ]
        total = terms[-1]
        for term in terms[-2::-1]:
            total = total * square + term
        return total

    sin = series(SIN_HALF, 1) * value
    cos = series(COS_HALF, 0)
    return 1.0 - sin * sin, sin * cos


def table_angle(turns, modulus):
    centred = ((turns + modulus // 2) & (modulus - 1)) - modulus // 2
    return cos_sin(centred.astype(jnp.float32), 2.0 * math.pi / modulus)


def complex_add(left, right):
    if left is None or right is None:
        return right if left is None else left
    return left[0] + right[0], left[1] + right[1]


def complex_sub(left, right):
    if right is None:
        return left
    if left is None:
        return -right[0], -right[1]
    return left[0] - right[0], left[1] - right[1]


def rotated(value, turn, size):
    if value is None:
        return None
    real, imag = value
    turn = turn % size
    if turn == 0:
        return value
    if 4 * turn == size:
        return imag, -real
    if 2 * turn == size:
        return -real, -imag
    if 4 * turn == 3 * size:
        return -imag, real
    cos = math.cos(2.0 * math.pi * turn / size)
    sin = math.sin(2.0 * math.pi * turn / size)
    return real * cos + imag * sin, imag * cos - real * sin


def fourier(values):
    size = len(values)
    if size == 1:
        return values
    even = fourier(values[0::2])
    odd = fourier(values[1::2])
    odd = [rotated(value, turn, size) for turn, value in enumerate(odd)]
    return [complex_add(a, b) for a, b in zip(even, odd)] + [
        complex_sub(a, b) for a, b in zip(even, odd)
    ]


def iota(shape, dim):
    return lax.broadcasted_iota(jnp.int32, shape, dim)


def far_field_kernel(slabs, groups, near, phase, out, *scratch):
    (
        plain, code, both, lens, prop, field, halves, bands, vert, sums, cols, got, mid,
        turned, twiddle, between, coarse_table, local_sem, send_sem, recv_sem, col_send, col_recv,
        met_sem,
    ) = scratch
    steps, lat_dev, width = phase.shape
    _, rows, points = prop.shape
    devices = slabs * groups
    angles = AV // devices
    total_rows = lat_dev * slabs
    modulus = 2 * total_rows
    fine = modulus // rows
    band = bands.shape[2] // 2
    slab = lax.axis_index("slab")
    grp = lax.axis_index("grp")
    me = slab * groups + grp
    peers = sorted(range(1, groups), key=lambda step: (2 * step != groups, step))

    def signal(semaphore, device):
        pl.semaphore_signal(
            semaphore, inc=1, device_id=device, device_id_type=pl.DeviceIdType.MESH
        )

    barrier = pltpu.get_barrier_semaphore()
    bits = slabs.bit_length() - 1
    for step in peers:
        signal(barrier, (slab, grp ^ step))
    for bit in range(bits):
        signal(barrier, (slab ^ (1 << bit), grp))

    def pass_on(bit):
        if bit > 0:
            pl.semaphore_wait(met_sem.at[bit - 1], 1)
        if bit < bits:
            signal(met_sem.at[bit], (slab ^ (1 << bit), grp))

    def rows_of(peer):
        return pl.ds(pl.multiple_of(peer * rows, rows), rows)

    def place_of(peer):
        return pl.ds(pl.multiple_of(peer * width, width), width)

    entrance_part = both.at[:, :, place_of(grp)]
    load_phase = [
        pltpu.make_async_copy(phase.at[k], plain.at[k], local_sem.at[k]) for k in range(steps)
    ]
    for copy in load_phase:
        copy.start()
    own_field = pltpu.make_async_copy(
        near.at[:, rows_of(grp)], entrance_part, local_sem.at[steps]
    )
    own_field.start()
    pl.semaphore_wait(barrier, groups - 1 + bits)

    def remote(source, target, slot, step):
        return pltpu.make_async_remote_copy(
            src_ref=source,
            dst_ref=target,
            send_sem=send_sem.at[slot, step],
            recv_sem=recv_sem.at[slot, step],
            device_id=(slab, grp ^ step),
            device_id_type=pl.DeviceIdType.MESH,
        )

    send_field = {
        step: remote(near.at[:, rows_of(grp ^ step)], entrance_part, steps, step)
        for step in peers
    }
    send_lens = [
        {
            step: remote(
                code.at[k, rows_of(grp ^ step)], lens.at[k, :, place_of(grp)], k, step
            )
            for step in peers
        }
        for k in range(steps)
    ]
    for step in peers:
        send_field[step].start()
    pass_on(0)

    own_lens = []
    for k in range(steps):
        load_phase[k].wait()

        def encode(index, carry):
            part = pl.ds(pl.multiple_of(index * 32, 32), 32)
            code[k, part] = jnp.exp(plain[k, part] * (PHASE_CODE * math.log(2.0))).astype(
                jnp.bfloat16
            )
            return carry

        lax.fori_loop(0, lat_dev // 32, encode, 0)
        own_lens.append(
            pltpu.make_async_copy(
                code.at[k, rows_of(grp)], lens.at[k, :, place_of(grp)], local_sem.at[k]
            )
        )
        own_lens[k].start()

    gain = 1.0 / math.sqrt(points)
    tall = 32

    def make_band(index, carry):
        start = pl.multiple_of(index * tall, tall)
        offset = iota((tall, band), 1) - iota((tall, band), 0) - start
        cos, sin = table_angle(offset * offset - points // 4, 2 * points)
        value = jnp.concatenate([cos, sin], axis=1) * gain
        parity = (iota((tall, 2 * band), 0) + iota((tall, 2 * band), 1)) & 1
        for odd in range(2):
            part = jnp.where(parity == odd, value, 0.0).astype(jnp.bfloat16)
            bands[odd, pl.ds(start, tall)] = part
            bands[odd, pl.ds(start + points, tall)] = part
        return carry

    lax.fori_loop(0, points // tall, make_band, 0)

    share = slabs * angles

    def make_vert(device, carry):
        row = lax.rem(device, groups) * (2 * share) + lax.div(device, groups) * angles
        row = pl.multiple_of(row, angles)
        for left in range(0, points, 512):
            shape = (angles, 512)
            angle = iota(shape, 0) + (device * angles - AV // 2)
            point = iota(shape, 1) + (left - points // 2)
            cos, sin = table_angle(angle * point, 2 * points)
            part = pl.ds(left, 512)
            vert[pl.ds(row, angles), part] = cos.astype(jnp.bfloat16)
            vert[pl.ds(pl.multiple_of(row + share, angles), angles), part] = sin.astype(
                jnp.bfloat16
            )
        return carry

    lax.fori_loop(0, devices, make_vert, 0)

    shape = (fine, rows)
    number = iota(shape, 0)
    cos, sin = table_angle(number * iota(shape, 1) - number * (total_rows // 2), modulus)
    scale = 1.0 / math.sqrt(total_rows * points)
    twiddle[0] = cos * scale
    twiddle[1] = sin * scale
    inner = 8
    outer = fine // inner
    shape = (outer * inner, rows)
    number = iota(shape, 0)
    cos, sin = table_angle((number // inner) * (number % inner), fine)
    between[0] = cos
    between[1] = sin
    coarse = AL // fine
    half = coarse // 2
    shape = (half, rows)
    for parity in range(2):
        number = 2 * iota(shape, 0) + parity
        cos, sin = table_angle(iota(shape, 1) * (number * fine - AL // 2), modulus)
        cos = cos.astype(jnp.bfloat16)
        sin = sin.astype(jnp.bfloat16)
        top = parity * coarse
        coarse_table[top : top + half, :rows] = cos
        coarse_table[top : top + half, rows:] = sin
        coarse_table[top + half : top + coarse, :rows] = -sin
        coarse_table[top + half : top + coarse, rows:] = cos

    middle = points // 2

    def propagate(source):
        def halve(index, carry):
            part = pl.ds(pl.multiple_of(index * 16, 16), 16)
            low, high = source(part)
            low = low.astype(jnp.float32)
            high = high.astype(jnp.float32)
            halves[0, part] = (low + high).astype(jnp.bfloat16)
            halves[1, part] = (low - high).astype(jnp.bfloat16)
            return carry

        lax.fori_loop(0, 2 * rows // 16, halve, 0)

        def block(index, carry):
            start = pl.multiple_of(lax.rem(points - index * band, points), band)
            even = matmul(halves[0], bands[0, pl.ds(start, middle)])
            odd = matmul(halves[1], bands[1, pl.ds(start, middle)])
            for upper in range(2):
                term = even - odd if upper else even + odd
                part = pl.ds(pl.multiple_of(index * band + upper * middle, band), band)
                prop[0, :, part] = (term[:rows, :band] - term[rows:, band:]).astype(jnp.bfloat16)
                prop[1, :, part] = (term[:rows, band:] + term[rows:, :band]).astype(jnp.bfloat16)
            return carry

        lax.fori_loop(0, middle // band, block, 0)

    def focus(k, peer):
        left = pl.multiple_of(peer * width, width)

        def part_of(index, carry):
            start = pl.multiple_of(index * 16, 16)
            part = pl.ds(left, width)
            real = prop[0, pl.ds(start, 16), part].astype(jnp.float32)
            imag = prop[1, pl.ds(start, 16), part].astype(jnp.float32)
            power = jnp.log(lens[k, pl.ds(start, 16), part].astype(jnp.float32))
            cos, sin = cos_sin(power, 1.0 / (PHASE_CODE * math.log(2.0)))
            field[pl.ds(start, 16), part] = (real * cos - imag * sin).astype(jnp.bfloat16)
            field[pl.ds(start + rows, 16), part] = (real * sin + imag * cos).astype(jnp.bfloat16)
            return carry

        lax.fori_loop(0, rows // 16, part_of, 0)

    for bit in range(bits):
        pass_on(bit + 1)
    for step in peers:
        send_field[step].wait_send()
        send_lens[0][step].start()
    own_field.wait()
    for step in peers:
        send_field[step].wait_recv()
    entrance = both.reshape(2 * rows, points)

    propagate(lambda part: (entrance[part, :middle], entrance[part, middle:]))
    for k in range(1, steps):
        own_lens[k - 1].wait()
        focus(k - 1, grp)
        for step in peers:
            send_lens[k - 1][step].wait_recv()
            send_lens[k - 1][step].wait_send()
            send_lens[k][step].start()
            focus(k - 1, grp ^ step)
        propagate(lambda part: (field[part, :middle], field[part, middle:]))

    def part_for(peer_slab, peer_grp):
        row = (peer_grp * slabs + peer_slab) * angles
        return cols.at[:, pl.ds(pl.multiple_of(row, angles), angles)]

    def column_copy(index, across):
        peer = (slab ^ index, grp ^ across)
        return pltpu.make_async_remote_copy(
            src_ref=part_for(*peer),
            dst_ref=got.at[me],
            send_sem=col_send.at[index, across],
            recv_sem=col_recv.at[index, across],
            device_id=peer,
            device_id_type=pl.DeviceIdType.MESH,
        )

    def over_slabs(across, action):
        def one(index, carry):
            action(column_copy(index, across))
            return carry

        lax.fori_loop(1 if across == 0 else 0, slabs, one, 0)

    def vertical(part, peer):
        return lax.dot_general(
            vert[part, place_of(peer)],
            field[:, place_of(peer)],
            (((1,), (1,)), ((), ())),
            preferred_element_type=jnp.float32,
        )

    own_lens[steps - 1].wait()
    for step in range(groups - 1):
        if step > 0:
            send_lens[steps - 1][step].wait_recv()
        peer = grp ^ step
        focus(steps - 1, peer)
        term = vertical(slice(None), peer)
        sums[...] = term if step == 0 else sums[...] + term
    peer = grp ^ (groups - 1)
    if groups > 1:
        send_lens[steps - 1][groups - 1].wait_recv()
    focus(steps - 1, peer)
    by_distance = sorted(range(groups), key=lambda step: (2 * step != groups, -step))
    for across in by_distance:
        target = grp ^ across
        part = pl.ds(pl.multiple_of(target * (2 * share), 2 * share), 2 * share)
        term = vertical(part, peer)
        if groups > 1:
            term = sums[part] + term
        place = pl.ds(pl.multiple_of(target * share, share), share)
        cols[0, place] = (term[:share, :rows] + term[share:, rows:]).astype(jnp.bfloat16)
        cols[1, place] = (term[:share, rows:] - term[share:, :rows]).astype(jnp.bfloat16)
        over_slabs(across, lambda copy: copy.start())
    own_cols = pltpu.make_async_copy(part_for(slab, grp), got.at[me], local_sem.at[0])
    own_cols.start()
    for step in peers:
        send_lens[steps - 1][step].wait_send()
    own_cols.wait()

    for across in reversed(by_distance):
        over_slabs(across, lambda copy: copy.wait_send())
        over_slabs(across, lambda copy: copy.wait_recv())
        for low_slab in range(outer // groups):
            low = low_slab * groups + (grp ^ across)
            values = [None] * inner
            for high in range(devices // outer):
                source = high * outer + low
                values[high] = (
                    got[source, 0].astype(jnp.float32),
                    got[source, 1].astype(jnp.float32),
                )
            for turn, (real, imag) in enumerate(fourier(values)):
                number = low * inner + turn
                if turn > 0:
                    cos = between[0, pl.ds(number, 1)]
                    sin = between[1, pl.ds(number, 1)]
                    real, imag = real * cos + imag * sin, imag * cos - real * sin
                mid[number, 0] = real
                mid[number, 1] = imag
    for turn in range(inner):
        values = [
            (mid[low * inner + turn, 0], mid[low * inner + turn, 1]) for low in range(outer)
        ]
        for high, (real, imag) in enumerate(fourier(values)):
            number = high * inner + turn
            cos = twiddle[0, number : number + 1]
            sin = twiddle[1, number : number + 1]
            turned[0, pl.ds(number, angles, stride=fine)] = real * cos + imag * sin
            turned[1, pl.ds(number, angles, stride=fine)] = imag * cos - real * sin
    lanes = 2 * fine
    low_half = iota((coarse, lanes), 1) < fine
    table = coarse_table[...]
    right = jnp.concatenate([turned[c].astype(jnp.bfloat16) for c in range(2)], axis=1)
    results = lax.dot_general(
        table, right, (((1,), (1,)), ((), ())), preferred_element_type=jnp.float32
    )
    for pair in range(angles // 2):
        result = results[:, pair * lanes : (pair + 1) * lanes]
        even = result[:coarse]
        odd = result[coarse:]
        first = jnp.where(low_half, even, pltpu.roll(odd, fine, 1))
        second = jnp.where(low_half, pltpu.roll(even, fine, 1), odd)
        for c in range(2):
            for angle, value in ((2 * pair, first), (2 * pair + 1, second)):
                row = (c * angles + angle // 8 * 8) * half + angle % 8
                out[pl.ds(row, half, stride=8)] = value[c * half : (c + 1) * half]


def one_kernel(near_field, lens_phase):
    slabs = lax.axis_size("slab")
    groups = lax.axis_size("grp")
    devices = slabs * groups
    steps, lat_dev, width = lens_phase.shape
    points = width * groups
    rows = lat_dev // groups
    angles = AV // devices
    fine = 2 * lat_dev * slabs // rows
    coarse = AL // fine
    band = math.gcd(points, 256)
    bf16 = jnp.bfloat16

    def kernel(*refs):
        far_field_kernel(slabs, groups, *refs)

    out = pl.pallas_call(
        kernel,
        out_shape=jax.ShapeDtypeStruct((angles * coarse, 2 * fine), jnp.float32),
        in_specs=[pl.BlockSpec(memory_space=pl.ANY)] * 2,
        out_specs=pl.BlockSpec(memory_space=pltpu.VMEM),
        scratch_shapes=[
            pltpu.VMEM(lens_phase.shape, jnp.float32),
            pltpu.VMEM(lens_phase.shape, bf16),
            pltpu.VMEM((2, rows, points), bf16),
            pltpu.VMEM((steps, rows, points), bf16),
            pltpu.VMEM((2, rows, points), bf16),
            pltpu.VMEM((2 * rows, points), bf16),
            pltpu.VMEM((2, 2 * rows, points // 2), bf16),
            pltpu.VMEM((2, 2 * points, 2 * band), bf16),
            pltpu.VMEM((2 * AV, points), bf16),
            pltpu.VMEM((2 * AV, 2 * rows), jnp.float32),
            pltpu.VMEM((2, AV, rows), bf16),
            pltpu.VMEM((devices, 2, angles, rows), bf16),
            pltpu.VMEM((fine, 2, angles, rows), jnp.float32),
            pltpu.VMEM((2, angles * fine, rows), jnp.float32),
            pltpu.VMEM((2, fine, rows), jnp.float32),
            pltpu.VMEM((2, fine, rows), jnp.float32),
            pltpu.VMEM((2 * coarse, 2 * rows), bf16),
            pltpu.SemaphoreType.DMA((steps + 1,)),
            pltpu.SemaphoreType.DMA((steps + 1, groups)),
            pltpu.SemaphoreType.DMA((steps + 1, groups)),
            pltpu.SemaphoreType.DMA((slabs, groups)),
            pltpu.SemaphoreType.DMA((slabs, groups)),
            pltpu.SemaphoreType.REGULAR((slabs.bit_length(),)),
        ],
        compiler_params=pltpu.CompilerParams(
            collective_id=1, has_side_effects=True, vmem_limit_bytes=53 * 1024 * 1024
        ),
        name="far_field",
    )(near_field, lens_phase)
    out = out.reshape(2, angles // 8, coarse // 2, 8, 2 * fine)
    return jnp.transpose(out, (0, 1, 3, 2, 4)).reshape(2, angles, AL)


def fits_one_kernel(mesh, shape):
    slabs = mesh.shape["slab"]
    groups = mesh.shape["grp"]
    devices = slabs * groups
    _, total_rows, points = shape
    rows = total_rows // devices
    powers = all(size & (size - 1) == 0 for size in (slabs, groups, points, total_rows))
    return powers and slabs >= 4 and points >= 512 and rows == 128 and AV // devices == 16 and 2 * total_rows // rows == 64


def solution(mesh):
    spec = P(None, "slab", "grp")

    def far_field(near_field, lens_phase):
        body = one_kernel if fits_one_kernel(mesh, lens_phase.shape) else on_device
        return jax.shard_map(
            body,
            mesh=mesh,
            in_specs=(spec, spec),
            out_specs=P(None, ("slab", "grp"), None),
            check_vma=False,
        )(near_field, lens_phase)

    return far_field
```

```python
import math

import jax
import jax.numpy as jnp
from jax import lax
from jax.experimental import pallas as pl
from jax.experimental.pallas import tpu as pltpu
from jax.sharding import PartitionSpec as P

AV = 512
AL = 2048
PHASE_CODE = 40.0


def sincos(angle):
    half = 0.5 * angle
    sq = half * half
    sin = -1.0 / 39916800.0
    for term in (1.0 / 362880.0, -1.0 / 5040.0, 1.0 / 120.0, -1.0 / 6.0, 1.0):
        sin = sin * sq + term
    sin = sin * half
    cos = 1.0 / 479001600.0
    for term in (-1.0 / 3628800.0, 1.0 / 40320.0, -1.0 / 720.0, 1.0 / 24.0, -0.5, 1.0):
        cos = cos * sq + term
    return 1.0 - 2.0 * sin * sin, 2.0 * sin * cos


def unit_angle(turns, modulus):
    assert modulus & (modulus - 1) == 0
    centred = ((turns + modulus // 2) & (modulus - 1)) - modulus // 2
    return sincos(centred.astype(jnp.float32) * (2.0 * math.pi / modulus))


def count(size):
    return lax.optimization_barrier(jnp.arange(size, dtype=jnp.int32))


def phase_table(row_index, col_index, modulus):
    cos, sin = unit_angle(row_index[:, None] * col_index[None, :], modulus)
    return cos.astype(jnp.bfloat16), sin.astype(jnp.bfloat16)


def conjugate(table):
    cos, sin = table
    return jnp.stack([jnp.stack([cos, -sin]), jnp.stack([sin, cos])])


def propagator(points):
    band = math.gcd(points, 256)
    offset = count(points)[None, :] - count(band)[:, None]
    cos, sin = unit_angle(offset * offset - points // 4, 2 * points)
    gain = 1.0 / math.sqrt(points)

    def rolled(part):
        part = lax.optimization_barrier((part * gain).astype(jnp.bfloat16))
        twice = jnp.concatenate([part, part], axis=1)
        return jnp.concatenate(
            [
                lax.slice_in_dim(twice, points - start, 2 * points - start, axis=1)
                for start in range(0, points, band)
            ]
        )

    return rolled(cos), rolled(sin)


def matmul(left, right):
    return jnp.dot(left, right, preferred_element_type=jnp.float32)


def complex_product(both, table_cos, table_sin):
    rows = both.shape[0] // 2
    with_cos = matmul(both, table_cos)
    with_sin = matmul(both, table_sin)
    return with_cos[:rows] - with_sin[rows:], with_sin[:rows] + with_cos[rows:]


def exchange_kernel(groups, devices, source, target, send_sem, recv_sem, own_sem):
    me = lax.axis_index("slab") * groups + lax.axis_index("grp")
    barrier = pltpu.get_barrier_semaphore()

    def place(device):
        return (lax.div(device, groups), lax.rem(device, groups))

    def greet(step, carry):
        peer = lax.rem(me + step, devices)
        pl.semaphore_signal(
            barrier, inc=1, device_id=place(peer), device_id_type=pl.DeviceIdType.MESH
        )
        return carry

    lax.fori_loop(1, devices, greet, 0)
    pl.semaphore_wait(barrier, devices - 1)

    def block(step):
        peer = lax.rem(me + step, devices)
        return pltpu.make_async_remote_copy(
            src_ref=source.at[peer],
            dst_ref=target.at[me],
            send_sem=send_sem.at[step],
            recv_sem=recv_sem.at[step],
            device_id=place(peer),
            device_id_type=pl.DeviceIdType.MESH,
        )

    def send(step, carry):
        block(step).start()
        return carry

    def wait(step, carry):
        block(step).wait()
        return carry

    lax.fori_loop(1, devices, send, 0)
    own = pltpu.make_async_copy(source.at[me], target.at[me], own_sem)
    own.start()
    own.wait()
    lax.fori_loop(1, devices, wait, 0)


def exchange(blocks, groups):
    devices = blocks.shape[0]

    def kernel(*refs):
        exchange_kernel(groups, devices, *refs)

    return pl.pallas_call(
        kernel,
        out_shape=jax.ShapeDtypeStruct(blocks.shape, blocks.dtype),
        in_specs=[pl.BlockSpec(memory_space=pltpu.VMEM)],
        out_specs=pl.BlockSpec(memory_space=pltpu.VMEM),
        scratch_shapes=[
            pltpu.SemaphoreType.DMA((devices,)),
            pltpu.SemaphoreType.DMA((devices,)),
            pltpu.SemaphoreType.DMA,
        ],
        compiler_params=pltpu.CompilerParams(collective_id=0, has_side_effects=True),
        name="column_exchange",
    )(blocks)


def on_device(near_field, lens_phase):
    slab_count = lax.axis_size("slab")
    group_count = lax.axis_size("grp")
    devices = slab_count * group_count
    steps, lat_dev, width = lens_phase.shape
    points = width * group_count
    total_rows = lat_dev * slab_count
    rows = lat_dev // group_count
    angles = AV // devices
    coded = [jnp.exp2(lens_phase[k] * PHASE_CODE).astype(jnp.bfloat16) for k in range(steps)]
    blocks = jnp.transpose(near_field.reshape(2, group_count, rows, width), (1, 0, 2, 3))
    field = lax.all_to_all(blocks, "grp", split_axis=0, concat_axis=0, tiled=True)
    arrived = field
    moved = []
    for part in coded:
        part, arrived = lax.optimization_barrier((part, arrived))
        if not moved:
            field = arrived
        else:
            moved[-1] = arrived
        arrived = lax.all_to_all(part, "grp", split_axis=0, concat_axis=1, tiled=True)
        moved.append(arrived)
    coded = moved
    prop_cos, prop_sin = propagator(points)
    both = jnp.transpose(field, (1, 2, 0, 3)).reshape(2 * rows, points)
    for section in range(steps):
        real, imag = complex_product(both, prop_cos, prop_sin)
        real = real.astype(jnp.bfloat16).astype(jnp.float32)
        imag = imag.astype(jnp.bfloat16).astype(jnp.float32)
        phase = jnp.log2(coded[section].astype(jnp.float32)) * (1.0 / PHASE_CODE)
        lens_cos, lens_sin = sincos(phase)
        both = jnp.concatenate(
            [
                (real * lens_cos - imag * lens_sin).astype(jnp.bfloat16),
                (real * lens_sin + imag * lens_cos).astype(jnp.bfloat16),
            ]
        )
    vert_cos, vert_sin = phase_table(
        count(AV) - AV // 2, count(points) - points // 2, 2 * points
    )
    vert_cos, vert_sin = lax.optimization_barrier((vert_cos, vert_sin))
    with_cos = jnp.einsum("av,nv->an", vert_cos, both, preferred_element_type=jnp.float32)
    with_sin = jnp.einsum("av,nv->an", vert_sin, both, preferred_element_type=jnp.float32)
    col_real = (with_cos[:, :rows] + with_sin[:, rows:]).astype(jnp.bfloat16)
    col_imag = (with_cos[:, rows:] - with_sin[:, :rows]).astype(jnp.bfloat16)
    cols = jnp.stack([part.reshape(devices, angles, rows) for part in (col_real, col_imag)], axis=1)
    got = exchange(cols.reshape(devices, 2 * angles, rows), group_count)
    modulus = 2 * total_rows
    period = modulus // rows
    source = count(devices) - devices // 2
    fine = count(period)
    near = count(rows)
    coarse = count(AL // period)
    scale = 1.0 / math.sqrt(total_rows * points)
    got = got.reshape(devices, 2, angles, rows)
    weights = conjugate(phase_table(source, fine, period))
    mid = jnp.einsum("skam,kcsf->cafm", got, weights, preferred_element_type=jnp.float32)
    t_cos, t_sin = unit_angle(fine[:, None] * near[None, :], modulus)
    t_cos = t_cos * scale
    t_sin = t_sin * scale
    turned = jnp.stack([mid[0] * t_cos + mid[1] * t_sin, mid[1] * t_cos - mid[0] * t_sin])
    weights = conjugate(phase_table(near, coarse * period - AL // 2, modulus))
    out = jnp.einsum(
        "kafm,kcmd->cadf", turned.astype(jnp.bfloat16), weights, preferred_element_type=jnp.float32
    )
    return out.reshape(2, angles, AL)


SIN_HALF = (9.99999977e-01, -1.66666476e-01, 8.33289957e-03, -1.98008819e-04, 2.59045627e-06)
COS_HALF = (9.99999953e-01, -4.99999053e-01, 4.16635829e-02, -1.38536904e-03, 2.31536098e-05)


def cos_sin(value, scale):
    square = value * value

    def series(terms, start):
        terms = [
            math.sqrt(2.0) * term * (0.5 * scale) ** (2 * power + start)
            for power, term in enumerate(terms)
        ]
        total = terms[-1]
        for term in terms[-2::-1]:
            total = total * square + term
        return total

    sin = series(SIN_HALF, 1) * value
    cos = series(COS_HALF, 0)
    return 1.0 - sin * sin, sin * cos


def table_angle(turns, modulus):
    centred = ((turns + modulus // 2) & (modulus - 1)) - modulus // 2
    return cos_sin(centred.astype(jnp.float32), 2.0 * math.pi / modulus)


def complex_add(left, right):
    if left is None or right is None:
        return right if left is None else left
    return left[0] + right[0], left[1] + right[1]


def complex_sub(left, right):
    if right is None:
        return left
    if left is None:
        return -right[0], -right[1]
    return left[0] - right[0], left[1] - right[1]


def rotated(value, turn, size):
    if value is None:
        return None
    real, imag = value
    turn = turn % size
    if turn == 0:
        return value
    if 4 * turn == size:
        return imag, -real
    if 2 * turn == size:
        return -real, -imag
    if 4 * turn == 3 * size:
        return -imag, real
    cos = math.cos(2.0 * math.pi * turn / size)
    sin = math.sin(2.0 * math.pi * turn / size)
    return real * cos + imag * sin, imag * cos - real * sin


def fourier(values):
    size = len(values)
    if size == 1:
        return values
    even = fourier(values[0::2])
    odd = fourier(values[1::2])
    odd = [rotated(value, turn, size) for turn, value in enumerate(odd)]
    return [complex_add(a, b) for a, b in zip(even, odd)] + [
        complex_sub(a, b) for a, b in zip(even, odd)
    ]


def iota(shape, dim):
    return lax.broadcasted_iota(jnp.int32, shape, dim)


def far_field_kernel(slabs, groups, near, phase, out, *scratch):
    (
        plain, code, both, lens, prop, field, halves, bands, vert, sums, cols, got, mid,
        turned, twiddle, between, coarse_table, local_sem, send_sem, recv_sem, col_send, col_recv,
        met_sem,
    ) = scratch
    steps, lat_dev, width = phase.shape
    _, rows, points = prop.shape
    devices = slabs * groups
    angles = AV // devices
    total_rows = lat_dev * slabs
    modulus = 2 * total_rows
    fine = modulus // rows
    band = bands.shape[2] // 2
    slab = lax.axis_index("slab")
    grp = lax.axis_index("grp")
    me = slab * groups + grp
    peers = sorted(range(1, groups), key=lambda step: (2 * step != groups, step))

    def signal(semaphore, device):
        pl.semaphore_signal(
            semaphore, inc=1, device_id=device, device_id_type=pl.DeviceIdType.MESH
        )

    barrier = pltpu.get_barrier_semaphore()
    bits = slabs.bit_length() - 1
    for step in peers:
        signal(barrier, (slab, grp ^ step))
    for bit in range(bits):
        signal(barrier, (slab ^ (1 << bit), grp))

    def pass_on(bit):
        if bit > 0:
            pl.semaphore_wait(met_sem.at[bit - 1], 1)
        if bit < bits:
            signal(met_sem.at[bit], (slab ^ (1 << bit), grp))

    def rows_of(peer):
        return pl.ds(pl.multiple_of(peer * rows, rows), rows)

    def place_of(peer):
        return pl.ds(pl.multiple_of(peer * width, width), width)

    entrance_part = both.at[:, :, place_of(grp)]
    load_phase = [
        pltpu.make_async_copy(phase.at[k], plain.at[k], local_sem.at[k]) for k in range(steps)
    ]
    for copy in load_phase:
        copy.start()
    own_field = pltpu.make_async_copy(
        near.at[:, rows_of(grp)], entrance_part, local_sem.at[steps]
    )
    own_field.start()
    pl.semaphore_wait(barrier, groups - 1 + bits)

    def remote(source, target, slot, step):
        return pltpu.make_async_remote_copy(
            src_ref=source,
            dst_ref=target,
            send_sem=send_sem.at[slot, step],
            recv_sem=recv_sem.at[slot, step],
            device_id=(slab, grp ^ step),
            device_id_type=pl.DeviceIdType.MESH,
        )

    send_field = {
        step: remote(near.at[:, rows_of(grp ^ step)], entrance_part, steps, step)
        for step in peers
    }
    send_lens = [
        {
            step: remote(
                code.at[k, rows_of(grp ^ step)], lens.at[k, :, place_of(grp)], k, step
            )
            for step in peers
        }
        for k in range(steps)
    ]
    for step in peers:
        send_field[step].start()
    pass_on(0)

    own_lens = []
    for k in range(steps):
        load_phase[k].wait()

        def encode(index, carry):
            part = pl.ds(pl.multiple_of(index * 32, 32), 32)
            code[k, part] = jnp.exp(plain[k, part] * (PHASE_CODE * math.log(2.0))).astype(
                jnp.bfloat16
            )
            return carry

        lax.fori_loop(0, lat_dev // 32, encode, 0)
        own_lens.append(
            pltpu.make_async_copy(
                code.at[k, rows_of(grp)], lens.at[k, :, place_of(grp)], local_sem.at[k]
            )
        )
        own_lens[k].start()

    gain = 1.0 / math.sqrt(points)
    tall = 32

    def make_band(index, carry):
        start = pl.multiple_of(index * tall, tall)
        offset = iota((tall, band), 1) - iota((tall, band), 0) - start
        cos, sin = table_angle(offset * offset - points // 4, 2 * points)
        value = jnp.concatenate([cos, sin], axis=1) * gain
        parity = (iota((tall, 2 * band), 0) + iota((tall, 2 * band), 1)) & 1
        for odd in range(2):
            part = jnp.where(parity == odd, value, 0.0).astype(jnp.bfloat16)
            bands[odd, pl.ds(start, tall)] = part
            bands[odd, pl.ds(start + points, tall)] = part
        return carry

    lax.fori_loop(0, points // tall, make_band, 0)

    share = slabs * angles

    def make_vert(device, carry):
        row = lax.rem(device, groups) * (2 * share) + lax.div(device, groups) * angles
        row = pl.multiple_of(row, angles)
        for left in range(0, points, 512):
            shape = (angles, 512)
            angle = iota(shape, 0) + (device * angles - AV // 2)
            point = iota(shape, 1) + (left - points // 2)
            cos, sin = table_angle(angle * point, 2 * points)
            part = pl.ds(left, 512)
            vert[pl.ds(row, angles), part] = cos.astype(jnp.bfloat16)
            vert[pl.ds(pl.multiple_of(row + share, angles), angles), part] = sin.astype(
                jnp.bfloat16
            )
        return carry

    lax.fori_loop(0, devices, make_vert, 0)

    shape = (fine, rows)
    number = iota(shape, 0)
    cos, sin = table_angle(number * iota(shape, 1) - number * (total_rows // 2), modulus)
    scale = 1.0 / math.sqrt(total_rows * points)
    twiddle[0] = cos * scale
    twiddle[1] = sin * scale
    inner = 8
    outer = fine // inner
    shape = (outer * inner, rows)
    number = iota(shape, 0)
    cos, sin = table_angle((number // inner) * (number % inner), fine)
    between[0] = cos
    between[1] = sin
    coarse = AL // fine
    half = coarse // 2
    shape = (half, rows)
    for parity in range(2):
        number = 2 * iota(shape, 0) + parity
        cos, sin = table_angle(iota(shape, 1) * (number * fine - AL // 2), modulus)
        cos = cos.astype(jnp.bfloat16)
        sin = sin.astype(jnp.bfloat16)
        top = parity * coarse
        coarse_table[top : top + half, :rows] = cos
        coarse_table[top : top + half, rows:] = sin
        coarse_table[top + half : top + coarse, :rows] = -sin
        coarse_table[top + half : top + coarse, rows:] = cos

    middle = points // 2

    def propagate(source):
        def halve(index, carry):
            part = pl.ds(pl.multiple_of(index * 16, 16), 16)
            low, high = source(part)
            low = low.astype(jnp.float32)
            high = high.astype(jnp.float32)
            halves[0, part] = (low + high).astype(jnp.bfloat16)
            halves[1, part] = (low - high).astype(jnp.bfloat16)
            return carry

        lax.fori_loop(0, 2 * rows // 16, halve, 0)

        def block(index, carry):
            start = pl.multiple_of(lax.rem(points - index * band, points), band)
            even = matmul(halves[0], bands[0, pl.ds(start, middle)])
            odd = matmul(halves[1], bands[1, pl.ds(start, middle)])
            for upper in range(2):
                term = even - odd if upper else even + odd
                part = pl.ds(pl.multiple_of(index * band + upper * middle, band), band)
                prop[0, :, part] = (term[:rows, :band] - term[rows:, band:]).astype(jnp.bfloat16)
                prop[1, :, part] = (term[:rows, band:] + term[rows:, :band]).astype(jnp.bfloat16)
            return carry

        lax.fori_loop(0, middle // band, block, 0)

    def focus(k, peer):
        left = pl.multiple_of(peer * width, width)

        def part_of(index, carry):
            start = pl.multiple_of(index * 16, 16)
            part = pl.ds(left, width)
            real = prop[0, pl.ds(start, 16), part].astype(jnp.float32)
            imag = prop[1, pl.ds(start, 16), part].astype(jnp.float32)
            power = jnp.log(lens[k, pl.ds(start, 16), part].astype(jnp.float32))
            cos, sin = cos_sin(power, 1.0 / (PHASE_CODE * math.log(2.0)))
            field[pl.ds(start, 16), part] = (real * cos - imag * sin).astype(jnp.bfloat16)
            field[pl.ds(start + rows, 16), part] = (real * sin + imag * cos).astype(jnp.bfloat16)
            return carry

        lax.fori_loop(0, rows // 16, part_of, 0)

    for bit in range(bits):
        pass_on(bit + 1)
    for step in peers:
        send_field[step].wait_send()
        send_lens[0][step].start()
    own_field.wait()
    for step in peers:
        send_field[step].wait_recv()
    entrance = both.reshape(2 * rows, points)

    propagate(lambda part: (entrance[part, :middle], entrance[part, middle:]))
    for k in range(1, steps):
        own_lens[k - 1].wait()
        focus(k - 1, grp)
        for step in peers:
            send_lens[k - 1][step].wait_recv()
            send_lens[k - 1][step].wait_send()
            send_lens[k][step].start()
            focus(k - 1, grp ^ step)
        propagate(lambda part: (field[part, :middle], field[part, middle:]))

    def part_for(peer_slab, peer_grp):
        row = (peer_grp * slabs + peer_slab) * angles
        return cols.at[:, pl.ds(pl.multiple_of(row, angles), angles)]

    def column_copy(index, across):
        peer = (slab ^ index, grp ^ across)
        return pltpu.make_async_remote_copy(
            src_ref=part_for(*peer),
            dst_ref=got.at[me],
            send_sem=col_send.at[index, across],
            recv_sem=col_recv.at[index, across],
            device_id=peer,
            device_id_type=pl.DeviceIdType.MESH,
        )

    def over_slabs(across, action):
        def one(index, carry):
            action(column_copy(slabs - 1 - index, across))
            return carry

        lax.fori_loop(0, slabs - 1 if across == 0 else slabs, one, 0)

    def vertical(part, peer):
        return lax.dot_general(
            vert[part, place_of(peer)],
            field[:, place_of(peer)],
            (((1,), (1,)), ((), ())),
            preferred_element_type=jnp.float32,
        )

    own_lens[steps - 1].wait()
    for step in range(groups - 1):
        if step > 0:
            send_lens[steps - 1][step].wait_recv()
        peer = grp ^ step
        focus(steps - 1, peer)
        term = vertical(slice(None), peer)
        sums[...] = term if step == 0 else sums[...] + term
    peer = grp ^ (groups - 1)
    if groups > 1:
        send_lens[steps - 1][groups - 1].wait_recv()
    focus(steps - 1, peer)
    by_distance = sorted(range(groups), key=lambda step: (2 * step != groups, -step))
    for across in by_distance:
        target = grp ^ across
        part = pl.ds(pl.multiple_of(target * (2 * share), 2 * share), 2 * share)
        term = vertical(part, peer)
        if groups > 1:
            term = sums[part] + term
        place = pl.ds(pl.multiple_of(target * share, share), share)
        cols[0, place] = (term[:share, :rows] + term[share:, rows:]).astype(jnp.bfloat16)
        cols[1, place] = (term[:share, rows:] - term[share:, :rows]).astype(jnp.bfloat16)
        over_slabs(across, lambda copy: copy.start())
    own_cols = pltpu.make_async_copy(part_for(slab, grp), got.at[me], local_sem.at[0])
    own_cols.start()
    for step in peers:
        send_lens[steps - 1][step].wait_send()
    own_cols.wait()

    for across in reversed(by_distance):
        over_slabs(across, lambda copy: copy.wait_send())
        over_slabs(across, lambda copy: copy.wait_recv())
        for low_slab in range(outer // groups):
            low = low_slab * groups + (grp ^ across)
            values = [None] * inner
            for high in range(devices // outer):
                source = high * outer + low
                values[high] = (
                    got[source, 0].astype(jnp.float32),
                    got[source, 1].astype(jnp.float32),
                )
            for turn, (real, imag) in enumerate(fourier(values)):
                number = low * inner + turn
                if turn > 0:
                    cos = between[0, pl.ds(number, 1)]
                    sin = between[1, pl.ds(number, 1)]
                    real, imag = real * cos + imag * sin, imag * cos - real * sin
                mid[number, 0] = real
                mid[number, 1] = imag
    for turn in range(inner):
        values = [
            (mid[low * inner + turn, 0], mid[low * inner + turn, 1]) for low in range(outer)
        ]
        for high, (real, imag) in enumerate(fourier(values)):
            number = high * inner + turn
            cos = twiddle[0, number : number + 1]
            sin = twiddle[1, number : number + 1]
            turned[0, pl.ds(number, angles, stride=fine)] = real * cos + imag * sin
            turned[1, pl.ds(number, angles, stride=fine)] = imag * cos - real * sin
    lanes = 2 * fine
    low_half = iota((coarse, lanes), 1) < fine
    table = coarse_table[...]
    right = jnp.concatenate([turned[c].astype(jnp.bfloat16) for c in range(2)], axis=1)
    results = lax.dot_general(
        table, right, (((1,), (1,)), ((), ())), preferred_element_type=jnp.float32
    )
    for pair in range(angles // 2):
        result = results[:, pair * lanes : (pair + 1) * lanes]
        even = result[:coarse]
        odd = result[coarse:]
        first = jnp.where(low_half, even, pltpu.roll(odd, fine, 1))
        second = jnp.where(low_half, pltpu.roll(even, fine, 1), odd)
        for c in range(2):
            for angle, value in ((2 * pair, first), (2 * pair + 1, second)):
                row = (c * angles + angle // 8 * 8) * half + angle % 8
                out[pl.ds(row, half, stride=8)] = value[c * half : (c + 1) * half]


def one_kernel(near_field, lens_phase):
    slabs = lax.axis_size("slab")
    groups = lax.axis_size("grp")
    devices = slabs * groups
    steps, lat_dev, width = lens_phase.shape
    points = width * groups
    rows = lat_dev // groups
    angles = AV // devices
    fine = 2 * lat_dev * slabs // rows
    coarse = AL // fine
    band = math.gcd(points, 256)
    bf16 = jnp.bfloat16

    def kernel(*refs):
        far_field_kernel(slabs, groups, *refs)

    out = pl.pallas_call(
        kernel,
        out_shape=jax.ShapeDtypeStruct((angles * coarse, 2 * fine), jnp.float32),
        in_specs=[pl.BlockSpec(memory_space=pl.ANY)] * 2,
        out_specs=pl.BlockSpec(memory_space=pltpu.VMEM),
        scratch_shapes=[
            pltpu.VMEM(lens_phase.shape, jnp.float32),
            pltpu.VMEM(lens_phase.shape, bf16),
            pltpu.VMEM((2, rows, points), bf16),
            pltpu.VMEM((steps, rows, points), bf16),
            pltpu.VMEM((2, rows, points), bf16),
            pltpu.VMEM((2 * rows, points), bf16),
            pltpu.VMEM((2, 2 * rows, points // 2), bf16),
            pltpu.VMEM((2, 2 * points, 2 * band), bf16),
            pltpu.VMEM((2 * AV, points), bf16),
            pltpu.VMEM((2 * AV, 2 * rows), jnp.float32),
            pltpu.VMEM((2, AV, rows), bf16),
            pltpu.VMEM((devices, 2, angles, rows), bf16),
            pltpu.VMEM((fine, 2, angles, rows), jnp.float32),
            pltpu.VMEM((2, angles * fine, rows), jnp.float32),
            pltpu.VMEM((2, fine, rows), jnp.float32),
            pltpu.VMEM((2, fine, rows), jnp.float32),
            pltpu.VMEM((2 * coarse, 2 * rows), bf16),
            pltpu.SemaphoreType.DMA((steps + 1,)),
            pltpu.SemaphoreType.DMA((steps + 1, groups)),
            pltpu.SemaphoreType.DMA((steps + 1, groups)),
            pltpu.SemaphoreType.DMA((slabs, groups)),
            pltpu.SemaphoreType.DMA((slabs, groups)),
            pltpu.SemaphoreType.REGULAR((slabs.bit_length(),)),
        ],
        compiler_params=pltpu.CompilerParams(
            collective_id=1, has_side_effects=True, vmem_limit_bytes=53 * 1024 * 1024
        ),
        name="far_field",
    )(near_field, lens_phase)
    out = out.reshape(2, angles // 8, coarse // 2, 8, 2 * fine)
    return jnp.transpose(out, (0, 1, 3, 2, 4)).reshape(2, angles, AL)


def fits_one_kernel(mesh, shape):
    slabs = mesh.shape["slab"]
    groups = mesh.shape["grp"]
    devices = slabs * groups
    _, total_rows, points = shape
    rows = total_rows // devices
    powers = all(size & (size - 1) == 0 for size in (slabs, groups, points, total_rows))
    return powers and slabs >= 4 and points >= 512 and rows == 128 and AV // devices == 16 and 2 * total_rows // rows == 64


def solution(mesh):
    spec = P(None, "slab", "grp")

    def far_field(near_field, lens_phase):
        body = one_kernel if fits_one_kernel(mesh, lens_phase.shape) else on_device
        return jax.shard_map(
            body,
            mesh=mesh,
            in_specs=(spec, spec),
            out_specs=P(None, ("slab", "grp"), None),
            check_vma=False,
        )(near_field, lens_phase)

    return far_field
```

```python
import math

import jax
import jax.numpy as jnp
from jax import lax
from jax.experimental import pallas as pl
from jax.experimental.pallas import tpu as pltpu
from jax.sharding import PartitionSpec as P

AV = 512
AL = 2048
PHASE_CODE = 40.0


def sincos(angle):
    half = 0.5 * angle
    sq = half * half
    sin = -1.0 / 39916800.0
    for term in (1.0 / 362880.0, -1.0 / 5040.0, 1.0 / 120.0, -1.0 / 6.0, 1.0):
        sin = sin * sq + term
    sin = sin * half
    cos = 1.0 / 479001600.0
    for term in (-1.0 / 3628800.0, 1.0 / 40320.0, -1.0 / 720.0, 1.0 / 24.0, -0.5, 1.0):
        cos = cos * sq + term
    return 1.0 - 2.0 * sin * sin, 2.0 * sin * cos


def unit_angle(turns, modulus):
    assert modulus & (modulus - 1) == 0
    centred = ((turns + modulus // 2) & (modulus - 1)) - modulus // 2
    return sincos(centred.astype(jnp.float32) * (2.0 * math.pi / modulus))


def count(size):
    return lax.optimization_barrier(jnp.arange(size, dtype=jnp.int32))


def phase_table(row_index, col_index, modulus):
    cos, sin = unit_angle(row_index[:, None] * col_index[None, :], modulus)
    return cos.astype(jnp.bfloat16), sin.astype(jnp.bfloat16)


def conjugate(table):
    cos, sin = table
    return jnp.stack([jnp.stack([cos, -sin]), jnp.stack([sin, cos])])


def propagator(points):
    band = math.gcd(points, 256)
    offset = count(points)[None, :] - count(band)[:, None]
    cos, sin = unit_angle(offset * offset - points // 4, 2 * points)
    gain = 1.0 / math.sqrt(points)

    def rolled(part):
        part = lax.optimization_barrier((part * gain).astype(jnp.bfloat16))
        twice = jnp.concatenate([part, part], axis=1)
        return jnp.concatenate(
            [
                lax.slice_in_dim(twice, points - start, 2 * points - start, axis=1)
                for start in range(0, points, band)
            ]
        )

    return rolled(cos), rolled(sin)


def matmul(left, right):
    return jnp.dot(left, right, preferred_element_type=jnp.float32)


def complex_product(both, table_cos, table_sin):
    rows = both.shape[0] // 2
    with_cos = matmul(both, table_cos)
    with_sin = matmul(both, table_sin)
    return with_cos[:rows] - with_sin[rows:], with_sin[:rows] + with_cos[rows:]


def exchange_kernel(groups, devices, source, target, send_sem, recv_sem, own_sem):
    me = lax.axis_index("slab") * groups + lax.axis_index("grp")
    barrier = pltpu.get_barrier_semaphore()

    def place(device):
        return (lax.div(device, groups), lax.rem(device, groups))

    def greet(step, carry):
        peer = lax.rem(me + step, devices)
        pl.semaphore_signal(
            barrier, inc=1, device_id=place(peer), device_id_type=pl.DeviceIdType.MESH
        )
        return carry

    lax.fori_loop(1, devices, greet, 0)
    pl.semaphore_wait(barrier, devices - 1)

    def block(step):
        peer = lax.rem(me + step, devices)
        return pltpu.make_async_remote_copy(
            src_ref=source.at[peer],
            dst_ref=target.at[me],
            send_sem=send_sem.at[step],
            recv_sem=recv_sem.at[step],
            device_id=place(peer),
            device_id_type=pl.DeviceIdType.MESH,
        )

    def send(step, carry):
        block(step).start()
        return carry

    def wait(step, carry):
        block(step).wait()
        return carry

    lax.fori_loop(1, devices, send, 0)
    own = pltpu.make_async_copy(source.at[me], target.at[me], own_sem)
    own.start()
    own.wait()
    lax.fori_loop(1, devices, wait, 0)


def exchange(blocks, groups):
    devices = blocks.shape[0]

    def kernel(*refs):
        exchange_kernel(groups, devices, *refs)

    return pl.pallas_call(
        kernel,
        out_shape=jax.ShapeDtypeStruct(blocks.shape, blocks.dtype),
        in_specs=[pl.BlockSpec(memory_space=pltpu.VMEM)],
        out_specs=pl.BlockSpec(memory_space=pltpu.VMEM),
        scratch_shapes=[
            pltpu.SemaphoreType.DMA((devices,)),
            pltpu.SemaphoreType.DMA((devices,)),
            pltpu.SemaphoreType.DMA,
        ],
        compiler_params=pltpu.CompilerParams(collective_id=0, has_side_effects=True),
        name="column_exchange",
    )(blocks)


def on_device(near_field, lens_phase):
    slab_count = lax.axis_size("slab")
    group_count = lax.axis_size("grp")
    devices = slab_count * group_count
    steps, lat_dev, width = lens_phase.shape
    points = width * group_count
    total_rows = lat_dev * slab_count
    rows = lat_dev // group_count
    angles = AV // devices
    coded = [jnp.exp2(lens_phase[k] * PHASE_CODE).astype(jnp.bfloat16) for k in range(steps)]
    blocks = jnp.transpose(near_field.reshape(2, group_count, rows, width), (1, 0, 2, 3))
    field = lax.all_to_all(blocks, "grp", split_axis=0, concat_axis=0, tiled=True)
    arrived = field
    moved = []
    for part in coded:
        part, arrived = lax.optimization_barrier((part, arrived))
        if not moved:
            field = arrived
        else:
            moved[-1] = arrived
        arrived = lax.all_to_all(part, "grp", split_axis=0, concat_axis=1, tiled=True)
        moved.append(arrived)
    coded = moved
    prop_cos, prop_sin = propagator(points)
    both = jnp.transpose(field, (1, 2, 0, 3)).reshape(2 * rows, points)
    for section in range(steps):
        real, imag = complex_product(both, prop_cos, prop_sin)
        real = real.astype(jnp.bfloat16).astype(jnp.float32)
        imag = imag.astype(jnp.bfloat16).astype(jnp.float32)
        phase = jnp.log2(coded[section].astype(jnp.float32)) * (1.0 / PHASE_CODE)
        lens_cos, lens_sin = sincos(phase)
        both = jnp.concatenate(
            [
                (real * lens_cos - imag * lens_sin).astype(jnp.bfloat16),
                (real * lens_sin + imag * lens_cos).astype(jnp.bfloat16),
            ]
        )
    vert_cos, vert_sin = phase_table(
        count(AV) - AV // 2, count(points) - points // 2, 2 * points
    )
    vert_cos, vert_sin = lax.optimization_barrier((vert_cos, vert_sin))
    with_cos = jnp.einsum("av,nv->an", vert_cos, both, preferred_element_type=jnp.float32)
    with_sin = jnp.einsum("av,nv->an", vert_sin, both, preferred_element_type=jnp.float32)
    col_real = (with_cos[:, :rows] + with_sin[:, rows:]).astype(jnp.bfloat16)
    col_imag = (with_cos[:, rows:] - with_sin[:, :rows]).astype(jnp.bfloat16)
    cols = jnp.stack([part.reshape(devices, angles, rows) for part in (col_real, col_imag)], axis=1)
    got = exchange(cols.reshape(devices, 2 * angles, rows), group_count)
    modulus = 2 * total_rows
    period = modulus // rows
    source = count(devices) - devices // 2
    fine = count(period)
    near = count(rows)
    coarse = count(AL // period)
    scale = 1.0 / math.sqrt(total_rows * points)
    got = got.reshape(devices, 2, angles, rows)
    weights = conjugate(phase_table(source, fine, period))
    mid = jnp.einsum("skam,kcsf->cafm", got, weights, preferred_element_type=jnp.float32)
    t_cos, t_sin = unit_angle(fine[:, None] * near[None, :], modulus)
    t_cos = t_cos * scale
    t_sin = t_sin * scale
    turned = jnp.stack([mid[0] * t_cos + mid[1] * t_sin, mid[1] * t_cos - mid[0] * t_sin])
    weights = conjugate(phase_table(near, coarse * period - AL // 2, modulus))
    out = jnp.einsum(
        "kafm,kcmd->cadf", turned.astype(jnp.bfloat16), weights, preferred_element_type=jnp.float32
    )
    return out.reshape(2, angles, AL)


SIN_HALF = (9.99999977e-01, -1.66666476e-01, 8.33289957e-03, -1.98008819e-04, 2.59045627e-06)
COS_HALF = (9.99999953e-01, -4.99999053e-01, 4.16635829e-02, -1.38536904e-03, 2.31536098e-05)


def cos_sin(value, scale):
    square = value * value

    def series(terms, start):
        terms = [
            math.sqrt(2.0) * term * (0.5 * scale) ** (2 * power + start)
            for power, term in enumerate(terms)
        ]
        total = terms[-1]
        for term in terms[-2::-1]:
            total = total * square + term
        return total

    sin = series(SIN_HALF, 1) * value
    cos = series(COS_HALF, 0)
    return 1.0 - sin * sin, sin * cos


def table_angle(turns, modulus):
    centred = ((turns + modulus // 2) & (modulus - 1)) - modulus // 2
    return cos_sin(centred.astype(jnp.float32), 2.0 * math.pi / modulus)


def complex_add(left, right):
    if left is None or right is None:
        return right if left is None else left
    return left[0] + right[0], left[1] + right[1]


def complex_sub(left, right):
    if right is None:
        return left
    if left is None:
        return -right[0], -right[1]
    return left[0] - right[0], left[1] - right[1]


def rotated(value, turn, size):
    if value is None:
        return None
    real, imag = value
    turn = turn % size
    if turn == 0:
        return value
    if 4 * turn == size:
        return imag, -real
    if 2 * turn == size:
        return -real, -imag
    if 4 * turn == 3 * size:
        return -imag, real
    cos = math.cos(2.0 * math.pi * turn / size)
    sin = math.sin(2.0 * math.pi * turn / size)
    return real * cos + imag * sin, imag * cos - real * sin


def fourier(values):
    size = len(values)
    if size == 1:
        return values
    even = fourier(values[0::2])
    odd = fourier(values[1::2])
    odd = [rotated(value, turn, size) for turn, value in enumerate(odd)]
    return [complex_add(a, b) for a, b in zip(even, odd)] + [
        complex_sub(a, b) for a, b in zip(even, odd)
    ]


def iota(shape, dim):
    return lax.broadcasted_iota(jnp.int32, shape, dim)


def far_field_kernel(slabs, groups, near, phase, out, *scratch):
    (
        plain, code, both, lens, prop, field, halves, bands, vert, sums, cols, got, mid,
        turned, twiddle, between, coarse_table, local_sem, send_sem, recv_sem, col_send, col_recv,
        met_sem,
    ) = scratch
    steps, lat_dev, width = phase.shape
    _, rows, points = prop.shape
    devices = slabs * groups
    angles = AV // devices
    total_rows = lat_dev * slabs
    modulus = 2 * total_rows
    fine = modulus // rows
    band = bands.shape[2] // 2
    slab = lax.axis_index("slab")
    grp = lax.axis_index("grp")
    me = slab * groups + grp
    peers = sorted(range(1, groups), key=lambda step: (2 * step != groups, step))

    def signal(semaphore, device):
        pl.semaphore_signal(
            semaphore, inc=1, device_id=device, device_id_type=pl.DeviceIdType.MESH
        )

    barrier = pltpu.get_barrier_semaphore()
    bits = slabs.bit_length() - 1
    for step in peers:
        signal(barrier, (slab, grp ^ step))
    for bit in range(bits):
        signal(barrier, (slab ^ (1 << bit), grp))

    def pass_on(bit):
        if bit > 0:
            pl.semaphore_wait(met_sem.at[bit - 1], 1)
        if bit < bits:
            signal(met_sem.at[bit], (slab ^ (1 << bit), grp))

    def rows_of(peer):
        return pl.ds(pl.multiple_of(peer * rows, rows), rows)

    def place_of(peer):
        return pl.ds(pl.multiple_of(peer * width, width), width)

    entrance_part = both.at[:, :, place_of(grp)]
    load_phase = [
        pltpu.make_async_copy(phase.at[k], plain.at[k], local_sem.at[k]) for k in range(steps)
    ]
    for copy in load_phase:
        copy.start()
    own_field = pltpu.make_async_copy(
        near.at[:, rows_of(grp)], entrance_part, local_sem.at[steps]
    )
    own_field.start()
    pl.semaphore_wait(barrier, groups - 1 + bits)

    def remote(source, target, slot, step):
        return pltpu.make_async_remote_copy(
            src_ref=source,
            dst_ref=target,
            send_sem=send_sem.at[slot, step],
            recv_sem=recv_sem.at[slot, step],
            device_id=(slab, grp ^ step),
            device_id_type=pl.DeviceIdType.MESH,
        )

    send_field = {
        step: remote(near.at[:, rows_of(grp ^ step)], entrance_part, steps, step)
        for step in peers
    }
    send_lens = [
        {
            step: remote(
                code.at[k, rows_of(grp ^ step)], lens.at[k, :, place_of(grp)], k, step
            )
            for step in peers
        }
        for k in range(steps)
    ]
    for step in peers:
        send_field[step].start()
    pass_on(0)

    own_lens = []
    for k in range(steps):
        load_phase[k].wait()

        def encode(index, carry):
            part = pl.ds(pl.multiple_of(index * 32, 32), 32)
            code[k, part] = jnp.exp(plain[k, part] * (PHASE_CODE * math.log(2.0))).astype(
                jnp.bfloat16
            )
            return carry

        lax.fori_loop(0, lat_dev // 32, encode, 0)
        own_lens.append(
            pltpu.make_async_copy(
                code.at[k, rows_of(grp)], lens.at[k, :, place_of(grp)], local_sem.at[k]
            )
        )
        own_lens[k].start()

    gain = 1.0 / math.sqrt(points)
    tall = 32

    def make_band(index, carry):
        start = pl.multiple_of(index * tall, tall)
        offset = iota((tall, band), 1) - iota((tall, band), 0) - start
        cos, sin = table_angle(offset * offset - points // 4, 2 * points)
        value = jnp.concatenate([cos, sin], axis=1) * gain
        parity = (iota((tall, 2 * band), 0) + iota((tall, 2 * band), 1)) & 1
        for odd in range(2):
            part = jnp.where(parity == odd, value, 0.0).astype(jnp.bfloat16)
            bands[odd, pl.ds(start, tall)] = part
            bands[odd, pl.ds(start + points, tall)] = part
        return carry

    lax.fori_loop(0, points // tall, make_band, 0)

    share = slabs * angles

    def make_vert(device, carry):
        row = lax.rem(device, groups) * (2 * share) + lax.div(device, groups) * angles
        row = pl.multiple_of(row, angles)
        for left in range(0, points, 512):
            shape = (angles, 512)
            angle = iota(shape, 0) + (device * angles - AV // 2)
            point = iota(shape, 1) + (left - points // 2)
            cos, sin = table_angle(angle * point, 2 * points)
            part = pl.ds(left, 512)
            vert[pl.ds(row, angles), part] = cos.astype(jnp.bfloat16)
            vert[pl.ds(pl.multiple_of(row + share, angles), angles), part] = sin.astype(
                jnp.bfloat16
            )
        return carry

    lax.fori_loop(0, devices, make_vert, 0)

    shape = (fine, rows)
    number = iota(shape, 0)
    cos, sin = table_angle(number * iota(shape, 1) - number * (total_rows // 2), modulus)
    scale = 1.0 / math.sqrt(total_rows * points)
    twiddle[0] = cos * scale
    twiddle[1] = sin * scale
    inner = 8
    outer = fine // inner
    shape = (outer * inner, rows)
    number = iota(shape, 0)
    cos, sin = table_angle((number // inner) * (number % inner), fine)
    between[0] = cos
    between[1] = sin
    coarse = AL // fine
    half = coarse // 2
    shape = (half, rows)
    for parity in range(2):
        number = 2 * iota(shape, 0) + parity
        cos, sin = table_angle(iota(shape, 1) * (number * fine - AL // 2), modulus)
        cos = cos.astype(jnp.bfloat16)
        sin = sin.astype(jnp.bfloat16)
        top = parity * coarse
        coarse_table[top : top + half, :rows] = cos
        coarse_table[top : top + half, rows:] = sin
        coarse_table[top + half : top + coarse, :rows] = -sin
        coarse_table[top + half : top + coarse, rows:] = cos

    middle = points // 2

    def propagate(source):
        def halve(index, carry):
            part = pl.ds(pl.multiple_of(index * 16, 16), 16)
            low, high = source(part)
            low = low.astype(jnp.float32)
            high = high.astype(jnp.float32)
            halves[0, part] = (low + high).astype(jnp.bfloat16)
            halves[1, part] = (low - high).astype(jnp.bfloat16)
            return carry

        lax.fori_loop(0, 2 * rows // 16, halve, 0)

        def block(index, carry):
            start = pl.multiple_of(lax.rem(points - index * band, points), band)
            even = matmul(halves[0], bands[0, pl.ds(start, middle)])
            odd = matmul(halves[1], bands[1, pl.ds(start, middle)])
            for upper in range(2):
                term = even - odd if upper else even + odd
                part = pl.ds(pl.multiple_of(index * band + upper * middle, band), band)
                prop[0, :, part] = (term[:rows, :band] - term[rows:, band:]).astype(jnp.bfloat16)
                prop[1, :, part] = (term[:rows, band:] + term[rows:, :band]).astype(jnp.bfloat16)
            return carry

        lax.fori_loop(0, middle // band, block, 0)

    def focus(k, peer):
        left = pl.multiple_of(peer * width, width)

        def part_of(index, carry):
            start = pl.multiple_of(index * 16, 16)
            part = pl.ds(left, width)
            real = prop[0, pl.ds(start, 16), part].astype(jnp.float32)
            imag = prop[1, pl.ds(start, 16), part].astype(jnp.float32)
            power = jnp.log(lens[k, pl.ds(start, 16), part].astype(jnp.float32))
            cos, sin = cos_sin(power, 1.0 / (PHASE_CODE * math.log(2.0)))
            field[pl.ds(start, 16), part] = (real * cos - imag * sin).astype(jnp.bfloat16)
            field[pl.ds(start + rows, 16), part] = (real * sin + imag * cos).astype(jnp.bfloat16)
            return carry

        lax.fori_loop(0, rows // 16, part_of, 0)

    for bit in range(bits):
        pass_on(bit + 1)
    own_field.wait()
    for step in peers:
        send_field[step].wait_recv()
        send_field[step].wait_send()
        send_lens[0][step].start()
    entrance = both.reshape(2 * rows, points)

    propagate(lambda part: (entrance[part, :middle], entrance[part, middle:]))
    for k in range(1, steps):
        own_lens[k - 1].wait()
        focus(k - 1, grp)
        for step in peers:
            send_lens[k - 1][step].wait_recv()
            send_lens[k - 1][step].wait_send()
            send_lens[k][step].start()
            focus(k - 1, grp ^ step)
        propagate(lambda part: (field[part, :middle], field[part, middle:]))

    def part_for(peer_slab, peer_grp):
        row = (peer_grp * slabs + peer_slab) * angles
        return cols.at[:, pl.ds(pl.multiple_of(row, angles), angles)]

    def column_copy(index, across):
        peer = (slab ^ index, grp ^ across)
        return pltpu.make_async_remote_copy(
            src_ref=part_for(*peer),
            dst_ref=got.at[me],
            send_sem=col_send.at[index, across],
            recv_sem=col_recv.at[index, across],
            device_id=peer,
            device_id_type=pl.DeviceIdType.MESH,
        )

    def over_slabs(across, action):
        def one(index, carry):
            action(column_copy(slabs - 1 - index, across))
            return carry

        lax.fori_loop(0, slabs - 1 if across == 0 else slabs, one, 0)

    def vertical(part, peer):
        return lax.dot_general(
            vert[part, place_of(peer)],
            field[:, place_of(peer)],
            (((1,), (1,)), ((), ())),
            preferred_element_type=jnp.float32,
        )

    own_lens[steps - 1].wait()
    for step in range(groups - 1):
        if step > 0:
            send_lens[steps - 1][step].wait_recv()
        peer = grp ^ step
        focus(steps - 1, peer)
        term = vertical(slice(None), peer)
        sums[...] = term if step == 0 else sums[...] + term
    peer = grp ^ (groups - 1)
    if groups > 1:
        send_lens[steps - 1][groups - 1].wait_recv()
    focus(steps - 1, peer)
    by_distance = sorted(range(groups), key=lambda step: (2 * step != groups, -step))
    for across in by_distance:
        target = grp ^ across
        part = pl.ds(pl.multiple_of(target * (2 * share), 2 * share), 2 * share)
        term = vertical(part, peer)
        if groups > 1:
            term = sums[part] + term
        place = pl.ds(pl.multiple_of(target * share, share), share)
        cols[0, place] = (term[:share, :rows] + term[share:, rows:]).astype(jnp.bfloat16)
        cols[1, place] = (term[:share, rows:] - term[share:, :rows]).astype(jnp.bfloat16)
        over_slabs(across, lambda copy: copy.start())
    own_cols = pltpu.make_async_copy(part_for(slab, grp), got.at[me], local_sem.at[0])
    own_cols.start()
    for step in peers:
        send_lens[steps - 1][step].wait_send()
    own_cols.wait()

    for across in reversed(by_distance):
        over_slabs(across, lambda copy: copy.wait_send())
        over_slabs(across, lambda copy: copy.wait_recv())
        for low_slab in range(outer // groups):
            low = low_slab * groups + (grp ^ across)
            values = [None] * inner
            for high in range(devices // outer):
                source = high * outer + low
                values[high] = (
                    got[source, 0].astype(jnp.float32),
                    got[source, 1].astype(jnp.float32),
                )
            for turn, (real, imag) in enumerate(fourier(values)):
                number = low * inner + turn
                if turn > 0:
                    cos = between[0, pl.ds(number, 1)]
                    sin = between[1, pl.ds(number, 1)]
                    real, imag = real * cos + imag * sin, imag * cos - real * sin
                mid[number, 0] = real
                mid[number, 1] = imag
    for turn in range(inner):
        values = [
            (mid[low * inner + turn, 0], mid[low * inner + turn, 1]) for low in range(outer)
        ]
        for high, (real, imag) in enumerate(fourier(values)):
            number = high * inner + turn
            cos = twiddle[0, number : number + 1]
            sin = twiddle[1, number : number + 1]
            turned[0, pl.ds(number, angles, stride=fine)] = real * cos + imag * sin
            turned[1, pl.ds(number, angles, stride=fine)] = imag * cos - real * sin
    lanes = 2 * fine
    low_half = iota((coarse, lanes), 1) < fine
    table = coarse_table[...]
    right = jnp.concatenate([turned[c].astype(jnp.bfloat16) for c in range(2)], axis=1)
    results = lax.dot_general(
        table, right, (((1,), (1,)), ((), ())), preferred_element_type=jnp.float32
    )
    for pair in range(angles // 2):
        result = results[:, pair * lanes : (pair + 1) * lanes]
        even = result[:coarse]
        odd = result[coarse:]
        first = jnp.where(low_half, even, pltpu.roll(odd, fine, 1))
        second = jnp.where(low_half, pltpu.roll(even, fine, 1), odd)
        for c in range(2):
            for angle, value in ((2 * pair, first), (2 * pair + 1, second)):
                row = (c * angles + angle // 8 * 8) * half + angle % 8
                out[pl.ds(row, half, stride=8)] = value[c * half : (c + 1) * half]


def one_kernel(near_field, lens_phase):
    slabs = lax.axis_size("slab")
    groups = lax.axis_size("grp")
    devices = slabs * groups
    steps, lat_dev, width = lens_phase.shape
    points = width * groups
    rows = lat_dev // groups
    angles = AV // devices
    fine = 2 * lat_dev * slabs // rows
    coarse = AL // fine
    band = math.gcd(points, 256)
    bf16 = jnp.bfloat16

    def kernel(*refs):
        far_field_kernel(slabs, groups, *refs)

    out = pl.pallas_call(
        kernel,
        out_shape=jax.ShapeDtypeStruct((angles * coarse, 2 * fine), jnp.float32),
        in_specs=[pl.BlockSpec(memory_space=pl.ANY)] * 2,
        out_specs=pl.BlockSpec(memory_space=pltpu.VMEM),
        scratch_shapes=[
            pltpu.VMEM(lens_phase.shape, jnp.float32),
            pltpu.VMEM(lens_phase.shape, bf16),
            pltpu.VMEM((2, rows, points), bf16),
            pltpu.VMEM((steps, rows, points), bf16),
            pltpu.VMEM((2, rows, points), bf16),
            pltpu.VMEM((2 * rows, points), bf16),
            pltpu.VMEM((2, 2 * rows, points // 2), bf16),
            pltpu.VMEM((2, 2 * points, 2 * band), bf16),
            pltpu.VMEM((2 * AV, points), bf16),
            pltpu.VMEM((2 * AV, 2 * rows), jnp.float32),
            pltpu.VMEM((2, AV, rows), bf16),
            pltpu.VMEM((devices, 2, angles, rows), bf16),
            pltpu.VMEM((fine, 2, angles, rows), jnp.float32),
            pltpu.VMEM((2, angles * fine, rows), jnp.float32),
            pltpu.VMEM((2, fine, rows), jnp.float32),
            pltpu.VMEM((2, fine, rows), jnp.float32),
            pltpu.VMEM((2 * coarse, 2 * rows), bf16),
            pltpu.SemaphoreType.DMA((steps + 1,)),
            pltpu.SemaphoreType.DMA((steps + 1, groups)),
            pltpu.SemaphoreType.DMA((steps + 1, groups)),
            pltpu.SemaphoreType.DMA((slabs, groups)),
            pltpu.SemaphoreType.DMA((slabs, groups)),
            pltpu.SemaphoreType.REGULAR((slabs.bit_length(),)),
        ],
        compiler_params=pltpu.CompilerParams(
            collective_id=1, has_side_effects=True, vmem_limit_bytes=53 * 1024 * 1024
        ),
        name="far_field",
    )(near_field, lens_phase)
    out = out.reshape(2, angles // 8, coarse // 2, 8, 2 * fine)
    return jnp.transpose(out, (0, 1, 3, 2, 4)).reshape(2, angles, AL)


def fits_one_kernel(mesh, shape):
    slabs = mesh.shape["slab"]
    groups = mesh.shape["grp"]
    devices = slabs * groups
    _, total_rows, points = shape
    rows = total_rows // devices
    powers = all(size & (size - 1) == 0 for size in (slabs, groups, points, total_rows))
    return powers and slabs >= 4 and points >= 512 and rows == 128 and AV // devices == 16 and 2 * total_rows // rows == 64


def solution(mesh):
    spec = P(None, "slab", "grp")

    def far_field(near_field, lens_phase):
        body = one_kernel if fits_one_kernel(mesh, lens_phase.shape) else on_device
        return jax.shard_map(
            body,
            mesh=mesh,
            in_specs=(spec, spec),
            out_specs=P(None, ("slab", "grp"), None),
            check_vma=False,
        )(near_field, lens_phase)

    return far_field
```
